32 devices in a mesh: frame: 8 (over y, x, core), head: 4 (over z).
Axes of the slice: x: 2, y: 2, z: 4, core: 2. Of those that a mesh axis runs over, the one named last changes fastest.
Arguments:
- visual: bfloat16 [1024, 8192], P('frame'), may hold values from -6 to 6
- w_key: bfloat16 [8192, 1024], P(None, 'head'), may hold values from -0.0625 to 0.0625
- w_value: bfloat16 [8192, 1024], P(None, 'head'), may hold values from -0.0625 to 0.0625
- queries: float32 [256, 8192], P('frame', 'head'), may hold values from -100 to 100
- out_grad: float32 [256, 8192], P('frame', 'head'), may hold values from -6 to 6
Outputs:
- query_grad: float32 [256, 8192], P('frame', 'head')
- key_weight_grad: float32 [8192, 1024], P('frame', 'head')
- value_weight_grad: float32 [8192, 1024], P('frame', 'head')
- visual_grad: float32 [1024, 8192], P('frame', 'head')
The draws below stay inside these ranges and needn't reach their ends.
All inputs are finite; a program needn't handle non-finite values.
Results may differ from the reference program's by a relative error of at most 0.009.
Values sent between devices are 32-bit elements; how exact they have to be, the bound alone decides.
A program may use at most 128 MiB of HBM per device.

```python
import jax
import jax.numpy as jnp
from jax import lax

D = 8192
HEADS = 64
KV_HEADS = 8
HEAD_DIM = 128
VISUAL = 1024
TEXT = 256


def draw_queries(key, part):
    shape = (TEXT, HEADS * HEAD_DIM)
    return jnp.clip(jax.random.normal(jax.random.fold_in(key, 11), shape, jnp.float32), -6.0, 6.0)


def level_of(rng, extent, pieces, low, top_value):
    def one(position, blocks):
        steps = jax.random.uniform(jax.random.fold_in(jax.random.fold_in(rng, 6), position), (blocks,), jnp.float32, low / len(pieces), top_value / len(pieces))
        return jnp.repeat(jnp.exp(steps), extent[position] // blocks).reshape((-1,) + (1,) * (len(extent) - position - 1))

    gain = one(*pieces[0])
    for cut in pieces[1:]:
        gain = gain * one(*cut)
    return gain


def scatter_about(own_key, shape, width, reach, shards=(), kind=jnp.bfloat16):
    drawn = jax.random.normal(own_key, shape, jnp.float32) * width
    if len(shards) > 0:
        drawn = level_of(own_key, shape, shards, -0.22, 0.18) * drawn
    return jnp.clip(drawn, min=-reach, max=reach).astype(kind)


def setup_inputs(seed: int = 0) -> dict:
    splits = jax.random.split(jax.random.key(seed), 6)
    visual = scatter_about(splits[0], (VISUAL, D), 1.0, 6.0, ((0, 8),))
    w_key = scatter_about(splits[1], (D, KV_HEADS * HEAD_DIM), D ** -0.5, 0.0625, ((1, 4),))
    w_value = scatter_about(splits[2], (D, KV_HEADS * HEAD_DIM), D ** -0.5, 0.0625, ((1, 4),))
    queries = draw_queries(jax.random.fold_in(splits[5], 71), 0)
    out_grad = scatter_about(splits[4], (TEXT, HEADS * HEAD_DIM), 1.0, 6.0, ((0, 8), (1, 4)), jnp.float32)
    return {"visual": visual, "w_key": w_key, "w_value": w_value, "queries": queries, "out_grad": out_grad}


def one_group(operands):
    query_blk, grad_blk, key_blk, value_blk = operands
    factor = HEAD_DIM ** -0.5
    scores = jnp.einsum('sgd,nd->gsn', query_blk, key_blk, precision=lax.Precision.HIGHEST) * factor
    top_score = jnp.max(scores, axis=-1, keepdims=True)
    log_total = top_score + jnp.log(jnp.sum(jnp.exp(scores - top_score), axis=-1, keepdims=True))
    probs = jnp.exp(scores - log_total)
    dprob = jnp.einsum('sgd,nd->gsn', grad_blk, value_blk, precision=lax.Precision.HIGHEST)
    delta = jnp.sum(probs * dprob, axis=-1, keepdims=True)
    dscore = probs * (dprob - delta)
    query_part = jnp.einsum('gsn,nd->sgd', dscore, key_blk, precision=lax.Precision.HIGHEST) * factor
    key_part = jnp.einsum('gsn,sgd->nd', dscore, query_blk, precision=lax.Precision.HIGHEST) * factor
    value_part = jnp.einsum('gsn,sgd->nd', probs, grad_blk, precision=lax.Precision.HIGHEST)
    return query_part, key_part, value_part


def reference(visual, w_key, w_value, queries, out_grad):
    keys = jnp.dot(visual, w_key, preferred_element_type=jnp.float32)
    values = jnp.dot(visual, w_value, preferred_element_type=jnp.float32)
    per_group = HEADS // KV_HEADS
    query_heads = queries.reshape(TEXT, KV_HEADS, per_group, HEAD_DIM).transpose(1, 0, 2, 3)
    grad_heads = out_grad.reshape(TEXT, KV_HEADS, per_group, HEAD_DIM).transpose(1, 0, 2, 3)
    key_heads = keys.reshape(VISUAL, KV_HEADS, HEAD_DIM).transpose(1, 0, 2)
    value_heads = values.reshape(VISUAL, KV_HEADS, HEAD_DIM).transpose(1, 0, 2)
    query_part, key_part, value_part = lax.map(one_group, (query_heads, grad_heads, key_heads, value_heads))
    query_grad = query_part.transpose(1, 0, 2, 3).reshape(TEXT, HEADS * HEAD_DIM)
    key_grad = key_part.transpose(1, 0, 2).reshape(VISUAL, KV_HEADS * HEAD_DIM).astype(jnp.bfloat16)
    value_grad = value_part.transpose(1, 0, 2).reshape(VISUAL, KV_HEADS * HEAD_DIM).astype(jnp.bfloat16)
    key_weight_grad = jnp.dot(visual.T, key_grad, preferred_element_type=jnp.float32)
    value_weight_grad = jnp.dot(visual.T, value_grad, preferred_element_type=jnp.float32)
    visual_grad = jnp.dot(key_grad, w_key.T, preferred_element_type=jnp.float32) + jnp.dot(value_grad, w_value.T, preferred_element_type=jnp.float32)
    return query_grad, key_weight_grad, value_weight_grad, visual_grad
```

```python
import functools

import jax
import jax.numpy as jnp
from jax import lax
from jax.experimental import pallas as pl
from jax.experimental.pallas import tpu as pltpu
from jax.sharding import PartitionSpec as P

HEAD_DIM = 128
MESH = pl.DeviceIdType.MESH
CHUNKS = 8
TILES = 8
UNITS = (1, 1, 2, 2, 2)
FAR, NEAR = 4, 2
LAG, MIDDLE = 3, 10
F32, BF16 = jnp.float32, jnp.bfloat16
LANES = (((1,), (1,)), ((), ()))


def halves(a):
    high = a.astype(BF16)
    return high, (a - high.astype(F32)).astype(BF16)


def product(a, b, dims):
    (ah, al), (bh, bl) = a, b
    dot = functools.partial(
        lax.dot_general, dimension_numbers=(dims, ((), ())), preferred_element_type=F32
    )
    return dot(ah, bh) + (dot(ah, bl) + dot(al, bh))


def kernel(
    n, nh, vis_any, wk_any, wv_any, q_any, g_any, qg_out, kwg_out, vwg_out, vg_out,
    vis, q, g, wk, wv, visf, visl, vist, ql, gl, kvs, kvl, parts, pre, partl, kgs, agl, kgb,
    qgs, qgl, vgp, zz, wst, wx, kgz,
    in_sems, w_sem, q_sems, g_sems, kv_sems, v_sems, pre_sems, part_sems, qg_sems, ag_sems,
    on_sems, z_sems, ws_sems, wz_sems, wx_sems, kz_sems,
):
    me, my_head = lax.axis_index("frame"), lax.axis_index("head")
    rows, depth = vis.shape
    cols = wk.shape[1]
    kv_local = cols // HEAD_DIM
    text_part, width = ql.shape[1], ql.shape[2]
    split = q.shape[0] // text_part
    heads = width // HEAD_DIM
    share = n // kv_local
    dn, dh = depth // n, depth // nh
    chunk = depth // CHUNKS
    tile = dh // TILES
    factor = HEAD_DIM ** (-0.5)
    bounds = [0]
    for u in UNITS:
        bounds.append(bounds[-1] + u * dn // sum(UNITS))
    ahead = [0] + [NEAR] * (nh - 2) + [FAR]

    def frame_copy_of(src, dst, send_sem, recv_sem, target):
        return pltpu.make_async_remote_copy(
            src_ref=src, dst_ref=dst, send_sem=send_sem, recv_sem=recv_sem,
            device_id={"frame": target}, device_id_type=MESH,
        )

    def frame_copy(src, dst, sems, slot_send, slot_recv, target):
        return frame_copy_of(src, dst, sems.at[0, slot_send], sems.at[1, slot_recv], target)

    def head_copy(src, dst, send_sem, recv_sem, target):
        return pltpu.make_async_remote_copy(
            src_ref=src, dst_ref=dst, send_sem=send_sem, recv_sem=recv_sem,
            device_id={"head": target}, device_id_type=MESH,
        )

    def peer(k):
        return lax.rem(me + k, n)

    def source(k):
        return lax.rem(me + n - k, n)

    core, chip, chips = lax.rem(me, 2), me // 2, n // 2
    sibling = me + 1 - 2 * core

    def mate(j):
        return lax.rem(me + 2 * j, n)

    def mate_source(j):
        return lax.rem(me + n - 2 * j, n)

    sends = []

    def send(copy):
        copy.start()
        sends.append(copy)

    def spread(pick, land, sems):
        send(frame_copy(pick(sibling), land.at[me], sems, sibling, me, sibling))
        for j in range(1, chips):
            p = mate(j)
            send(frame_copy(pick(p), land.at[me], sems, p, me, p))

    def forward(land, sems, on):
        for j in range(1, chips):
            s = mate_source(j)
            frame_copy(land.at[s], land.at[s], sems, s, s, s).wait_recv()
            send(frame_copy_of(land.at[s], land.at[s], on.at[s], sems.at[1, s], sibling))

    def wait_rest(land, sems):
        frame_copy(land.at[sibling], land.at[sibling], sems, sibling, sibling, sibling).wait_recv()
        for j in range(1, chips):
            s = lax.rem(sibling + n - 2 * j, n)
            frame_copy(land.at[s], land.at[s], sems, s, s, sibling).wait_recv()

    def wait_all(land, sems):
        for k in range(1, n):
            s = source(k)
            frame_copy(land.at[s], land.at[s], sems, s, s, s).wait_recv()

    def to_vmem(src, dst, sem):
        copy = pltpu.make_async_copy(src, dst, sem)
        copy.start()
        return copy

    texts_in = [to_vmem(q_any, q, in_sems.at[0]), to_vmem(g_any, g, in_sems.at[1])]
    vis_in = to_vmem(vis_any, vis, in_sems.at[2])
    loads = [
        [
            to_vmem(src.at[pl.ds(c * chunk, chunk)], dst.at[pl.ds(c * chunk, chunk)], w_sem.at[i, c])
            for c in range(CHUNKS)
        ]
        for i, (src, dst) in enumerate(((wk_any, wk), (wv_any, wv)))
    ]

    barrier = pltpu.get_barrier_semaphore()
    for k in range(1, n):
        pl.semaphore_signal(barrier, inc=1, device_id={"frame": peer(k)}, device_id_type=MESH)
    for j in range(1, nh):
        pl.semaphore_signal(
            barrier, inc=1, device_id={"head": lax.rem(my_head + j, nh)}, device_id_type=MESH
        )
    pl.semaphore_wait(barrier, n + nh - 2)

    def text_at(p):
        part, block = lax.rem(p, split), p // split
        return (
            pl.ds(pl.multiple_of(part * text_part, text_part), text_part),
            pl.ds(pl.multiple_of(block * width, width), width),
        )

    for copy, src, dst, sems in ((texts_in[0], q, ql, q_sems), (texts_in[1], g, gl, g_sems)):
        copy.wait()
        for k in range(1, n):
            p = peer(k)
            send(frame_copy(src.at[text_at(p)], dst.at[me], sems, p, me, p))
        dst[me] = src[text_at(me)]

    vis_in.wait()
    for i, w in enumerate((wk, wv)):
        acc = jnp.zeros((rows, cols), F32)
        for c in range(CHUNKS):
            loads[i][c].wait()
            at = pl.ds(c * chunk, chunk)
            acc += jnp.dot(vis[:, at], w[at], preferred_element_type=F32)
        for a in range(kv_local):
            kvs[i, a] = acc[:, a * HEAD_DIM : (a + 1) * HEAD_DIM]
        spread(lambda p, i=i: kvs.at[i, p // share], kvl.at[i], kv_sems.at[i])
        kvl[i, me] = kvs[i, me // share]

    is_end = jnp.logical_or(my_head == 0, my_head == nh - 1)
    staged = [(t, c) for t in range(nh - 1, 0, -1) for c in range(ahead[t])]
    slots = wx.shape[1]
    tw = tile // n

    def slot_of(t, c):
        return c if t == nh - 1 else jnp.where(my_head == 0, c, NEAR + c)

    def stage_copy(k):
        t, c = staged[k]
        d = jnp.where(my_head == 0, t, nh - 1 - t)
        return head_copy(
            wst.at[k], wx.at[me, slot_of(t, c)], ws_sems.at[k], wz_sems.at[slot_of(t, c)], d
        )

    if staged:

        @pl.when(is_end)
        def _():
            for k, (t, c) in enumerate(staged):
                d = jnp.where(my_head == 0, t, nh - 1 - t)
                at = pl.ds(pl.multiple_of(d * dh + c * tile + me * tw, tw), tw)
                for i, w in enumerate((wk, wv)):
                    wst[k, i] = w[at].astype(F32)
                stage_copy(k).start()

    def turn_visual(i):
        at = slice(bounds[i], bounds[i + 1])
        for p in range(n):
            block = vis[:, p * dn + bounds[i] : p * dn + bounds[i + 1]]
            visf[p, at] = block.astype(F32).T
        visl[me, at] = visf[me, at]

    def send_visual(i):
        at = pl.ds(bounds[i], bounds[i + 1] - bounds[i])
        for k in range(1, n):
            p = peer(k)
            send(frame_copy(visf.at[p, at], visl.at[me, at], v_sems.at[i], p, me, p))

    def take_visual(i):
        at = pl.ds(bounds[i], bounds[i + 1] - bounds[i])
        for k in range(1, n):
            s = source(k)
            land = visl.at[s, at]
            frame_copy(land, land, v_sems.at[i], s, s, s).wait_recv()
        for s in range(n):
            vist[at, s * rows : (s + 1) * rows] = visl[s, at].astype(BF16)
        for j, out in enumerate((kwg_out, vwg_out)):
            out[at] = jnp.dot(vist[at], kgb[j], preferred_element_type=F32)

    turn_visual(0)
    send_visual(0)
    for i in range(1, len(UNITS)):
        turn_visual(i)

    forward(kvl.at[0], kv_sems.at[0], on_sems.at[0])
    wait_all(ql, q_sems)
    wait_rest(kvl.at[0], kv_sems.at[0])
    keys = kvl[0].reshape(n * rows, HEAD_DIM)
    texts = [slice(h * HEAD_DIM, (h + 1) * HEAD_DIM) for h in range(heads)]
    queries = [ql[:, :, at].reshape(n * text_part, HEAD_DIM) for at in texts]
    probs = []
    for query in queries:
        scores = lax.dot_general(
            keys, query, LANES, precision=lax.Precision.HIGHEST, preferred_element_type=F32
        ) * factor
        raw = jnp.exp(scores - jnp.max(scores, axis=0, keepdims=True))
        probs.append(raw * (1.0 / jnp.sum(raw, axis=0, keepdims=True)))

    forward(kvl.at[1], kv_sems.at[1], on_sems.at[1])
    wait_all(gl, g_sems)
    grads2 = [halves(gl[:, :, at].reshape(n * text_part, HEAD_DIM)) for at in texts]

    def total(terms):
        out = terms[0]
        for term in terms[1:]:
            out = out + term
        return out

    def exchange(i):
        return frame_copy_of(
            parts.at[i, 1 - core], pre.at[i], pre_sems.at[i, 0], pre_sems.at[i, 1], sibling
        )

    def give(i, part):
        part = part.reshape(chips, 2, rows, HEAD_DIM)
        for c in range(2):
            parts[i, c] = part[:, c]
        send(exchange(i))

    def pass_on(i):
        exchange(i).wait_recv()
        parts[i, core] += pre[i]
        for j in range(1, chips):
            p = mate(j)
            send(
                frame_copy(
                    parts.at[i, core, p // 2], partl.at[i, chip], part_sems.at[i], p // 2, chip, p
                )
            )
        partl[i, chip] = parts[i, core, chip]

    give(1, total([product(halves(p), g2, ((1,), (0,))) for p, g2 in zip(probs, grads2)]))

    wait_rest(kvl.at[1], kv_sems.at[1])
    values2 = halves(kvl[1].reshape(n * rows, HEAD_DIM))
    dscores2 = []
    for p, g2 in zip(probs, grads2):
        dprob = product(values2, g2, ((1,), (1,)))
        delta = jnp.sum(p * dprob, axis=0, keepdims=True)
        dscores2.append(halves(p * (dprob - delta)))
    pass_on(1)
    give(0, total([product(d2, halves(query), ((1,), (0,))) for d2, query in zip(dscores2, queries)]))
    keys_t = halves(keys.T)
    for d2, at in zip(dscores2, texts):
        query_term = product(keys_t, d2, ((1,), (0,))).T * factor
        qgs[:, :, at] = query_term.reshape(n, text_part, HEAD_DIM)
    pass_on(0)
    send_visual(1)

    low = [None, None]
    for i in (1, 0):
        for j in range(1, chips):
            s = mate_source(j)
            land = partl.at[i, s // 2]
            frame_copy(land, land, part_sems.at[i], s // 2, s // 2, s).wait_recv()
        for a in range(kv_local):
            column = total([partl[i, p] for p in range(a * share // 2, (a + 1) * share // 2)])
            if i == 0:
                column = column * factor
            kgs[i, :, a * HEAD_DIM : (a + 1) * HEAD_DIM] = column.astype(BF16).astype(F32)
        low[i] = kgs[i].astype(BF16)

    lead = jnp.where(2 * my_head < nh, 0, 1)

    def block_of(way, t):
        return jnp.where(way == 0, t, nh - 1 - t)

    def rank(way):
        return jnp.where(way == 0, my_head, nh - 1 - my_head)

    def visual_term(d, c):
        at = pl.ds(pl.multiple_of(d * dh + c * tile, tile), tile)
        vgp[d, c] = lax.dot_general(
            low[0], wk[at], LANES, preferred_element_type=F32
        ) + lax.dot_general(low[1], wv[at], LANES, preferred_element_type=F32)

    def onward_head(way):
        return jnp.clip(my_head + 1 - 2 * way, 0, nh - 1)

    def hop(way, d, c):
        return head_copy(
            vgp.at[d, c], zz.at[way, d, c], z_sems.at[way, 0, d, c], z_sems.at[way, 1, d, c],
            onward_head(way),
        )

    def starts(t, c):
        return 1 if c < ahead[t] else 0

    def relay(way, t, c):
        d, first = block_of(way, t), starts(t, c)

        @pl.when(jnp.logical_and(rank(way) < t, rank(way) >= first))
        def _():
            @pl.when(rank(way) > first)
            def _():
                hop(way, d, c).wait_recv()
                vgp[d, c] += zz[way, d, c]

            hop(way, d, c).start()

    def kg_hop(way, first):
        return head_copy(
            kgs if first else kgz.at[way], kgz.at[way], kz_sems.at[way, 0], kz_sems.at[way, 1],
            onward_head(way),
        )

    def relay_grads(way):
        @pl.when(rank(way) == 0)
        def _():
            kg_hop(way, True).start()

        @pl.when(rank(way) > 0)
        def _():
            kg_hop(way, False).wait_recv()

            @pl.when(rank(way) < nh - 1)
            def _():
                kg_hop(way, False).start()

    def gather_ahead():
        for j in range(slots):
            land = wx.at[me, j]
            head_copy(land, land, wz_sems.at[j], wz_sems.at[j], my_head).wait_recv()
        spread(lambda p: wx.at[me], wx, wx_sems)

    def add_ahead():
        forward(wx, wx_sems, on_sems.at[3])
        wait_rest(wx, wx_sems)
        for j in range(slots):
            from_right = jnp.where(is_end, jnp.where(my_head == 0, 1, 0), 1 if j >= NEAR else 0)
            c = jnp.where(is_end, j, j % NEAR)
            term = vgp[my_head, c]
            for i in range(2):
                block = wx[:, j, i].reshape(tile, cols).astype(BF16)
                term += lax.dot_general(
                    kgz[from_right, i].astype(BF16), block, LANES, preferred_element_type=F32
                )
            vgp[my_head, c] = term

    spread(lambda p: kgs, agl, ag_sems)
    agl[me] = kgs[...]
    for k in range(1, n):
        p = peer(k)
        send(frame_copy(qgs.at[p], qgl.at[me], qg_sems, p, me, p))
    qgl[me] = qgs[me]
    for i in range(2, len(UNITS)):
        send_visual(i)

    def middle():
        if staged:
            gather_ahead()
        forward(agl, ag_sems, on_sems.at[2])
        wait_rest(agl, ag_sems)
        for i in range(2):
            kgb[i] = agl[:, i].reshape(n * rows, cols).astype(BF16)
        take_visual(0)
        take_visual(1)

    order = [(t, c) for t in range(nh - 1, 0, -1) for c in range(TILES)]

    def visual_terms(way, t, c):
        @pl.when(rank(way) >= starts(t, c))
        def _():
            visual_term(block_of(way, t), c)

    for k in range(len(order) + LAG):
        if k < len(order):
            t, c = order[k]
            if 2 * t > nh - 1:
                visual_terms(lead, t, c)
                visual_terms(1 - lead, t, c)
            if k == FAR:
                if staged:
                    relay_grads(lead)
            relay(lead, t, c)
        if k >= LAG:
            if k - LAG == FAR and staged:
                relay_grads(1 - lead)
            relay(1 - lead, *order[k - LAG])
        if k == MIDDLE:
            middle()

    for i in range(2, len(UNITS)):
        take_visual(i)
    wait_all(qgl, qg_sems)
    for s in range(n):
        part, block = s % split, s // split
        qg_out[
            part * text_part : (part + 1) * text_part, block * width : (block + 1) * width
        ] = qgl[s]
    if staged:
        add_ahead()

    for c in range(TILES):
        at = slice(c * tile, (c + 1) * tile)
        vg_out[:, at] = vgp[my_head, c]
        for way in (lead, 1 - lead):
            t = rank(way)
            count = jnp.where(t == nh - 1, FAR, NEAR)

            @pl.when(t > jnp.where(c < count, 1, 0))
            def _():
                hop(way, my_head, c).wait_recv()
                vg_out[:, at] += zz[way, my_head, c]

    for way in (lead, 1 - lead):
        for t, c in order:

            @pl.when(jnp.logical_and(rank(way) < t, rank(way) >= starts(t, c)))
            def _():
                hop(way, block_of(way, t), c).wait_send()

        if staged:

            @pl.when(rank(way) < nh - 1)
            def _():
                kg_hop(way, True).wait_send()

    if staged:

        @pl.when(is_end)
        def _():
            for k in range(len(staged)):
                stage_copy(k).wait_send()

    for copy in sends:
        copy.wait_send()


def store(*refs):
    outs, sems = refs[len(refs) // 2 : -1], refs[-1]
    copies = [
        pltpu.make_async_copy(src, dst, sems.at[i]) for i, (src, dst) in enumerate(zip(refs, outs))
    ]
    for copy in copies:
        copy.start()
    for copy in copies:
        copy.wait()


def solution(mesh):
    n, nh = mesh.shape["frame"], mesh.shape["head"]

    def body(visual, w_key, w_value, queries, out_grad):
        rows, depth = visual.shape
        cols = w_key.shape[1]
        text, query_cols = queries.shape
        local_heads = query_cols // HEAD_DIM
        split = max(1, n // local_heads)
        part, width = text // split, query_cols * split // n
        vmem = pl.BlockSpec(memory_space=pltpu.VMEM)
        hbm = pl.BlockSpec(memory_space=pl.ANY)
        dn, dh = depth // n, depth // nh
        tile = dh // TILES
        slots = max(FAR, 2 * NEAR, 1)
        pairs = pltpu.SemaphoreType.DMA((2, n))
        dma = pltpu.SemaphoreType.DMA
        outs = pl.pallas_call(
            functools.partial(kernel, n, nh),
            out_shape=(
                pltpu.VMEM((text, query_cols), F32),
                pltpu.VMEM((dn, cols), F32),
                pltpu.VMEM((dn, cols), F32),
                pltpu.VMEM((rows, dh), F32),
            ),
            in_specs=[hbm] * 5,
            out_specs=(vmem,) * 4,
            scratch_shapes=[
                pltpu.VMEM((rows, depth), BF16),
                pltpu.VMEM((text, query_cols), F32),
                pltpu.VMEM((text, query_cols), F32),
                pltpu.VMEM((depth, cols), BF16),
                pltpu.VMEM((depth, cols), BF16),
                pltpu.VMEM((n, dn, rows), F32),
                pltpu.VMEM((n, dn, rows), F32),
                pltpu.VMEM((dn, n * rows), BF16),
                pltpu.VMEM((n, part, width), F32),
                pltpu.VMEM((n, part, width), F32),
                pltpu.VMEM((2, cols // HEAD_DIM, rows, HEAD_DIM), F32),
                pltpu.VMEM((2, n, rows, HEAD_DIM), F32),
                pltpu.VMEM((2, 2, n // 2, rows, HEAD_DIM), F32),
                pltpu.VMEM((2, n // 2, rows, HEAD_DIM), F32),
                pltpu.VMEM((2, n // 2, rows, HEAD_DIM), F32),
                pltpu.VMEM((2, rows, cols), F32),
                pltpu.VMEM((n, 2, rows, cols), F32),
                pltpu.VMEM((2, n * rows, cols), BF16),
                pltpu.VMEM((n, part, width), F32),
                pltpu.VMEM((n, part, width), F32),
                pltpu.VMEM((nh, TILES, rows, tile), F32),
                pltpu.VMEM((2, nh, TILES, rows, tile), F32),
                pltpu.VMEM((max(FAR + NEAR * (nh - 2), 1), 2, tile // n, cols), F32),
                pltpu.VMEM((n, slots, 2, tile // n, cols), F32),
                pltpu.VMEM((2, 2, rows, cols), F32),
                dma((3,)),
                dma((2, CHUNKS)),
                pairs, pairs,
                dma((2, 2, n)),
                dma((len(UNITS), 2, n)),
                dma((2, 2)),
                dma((2, 2, n // 2)),
                pairs, pairs,
                dma((4, n)),
                dma((2, 2, nh, TILES)),
                dma((max(FAR + NEAR * (nh - 2), 1),)),
                dma((slots,)),
                pairs,
                dma((2, 2)),
            ],
            compiler_params=pltpu.CompilerParams(
                collective_id=0, has_side_effects=True, vmem_limit_bytes=60000000
            ),
        )(visual, w_key, w_value, queries, out_grad)
        return pl.pallas_call(
            store,
            out_shape=tuple(jax.ShapeDtypeStruct(o.shape, o.dtype) for o in outs),
            in_specs=[vmem] * 4,
            out_specs=(hbm,) * 4,
            scratch_shapes=[dma((4,))],
            compiler_params=pltpu.CompilerParams(vmem_limit_bytes=1 << 20),
        )(*[pltpu.with_memory_space_constraint(o, pltpu.VMEM) for o in outs])

    return jax.shard_map(
        body,
        mesh=mesh,
        in_specs=(
            P("frame", None),
            P(None, "head"),
            P(None, "head"),
            P("frame", "head"),
            P("frame", "head"),
        ),
        out_specs=(P("frame", "head"), P("frame", "head"), P("frame", "head"), P("frame", "head")),
        check_vma=False,
    )
```

```python
import functools

import jax
import jax.numpy as jnp
from jax import lax
from jax.experimental import pallas as pl
from jax.experimental.pallas import tpu as pltpu
from jax.sharding import PartitionSpec as P

HEAD_DIM = 128
MESH = pl.DeviceIdType.MESH
CHUNKS = 8
TILES = 8
UNITS = (2, 1, 1, 2, 2)
FAR, NEAR = 4, 2
LAG = 3
F32, BF16 = jnp.float32, jnp.bfloat16
LANES = (((1,), (1,)), ((), ()))


def halves(a):
    high = a.astype(BF16)
    return high, (a - high.astype(F32)).astype(BF16)


def product(a, b, dims):
    (ah, al), (bh, bl) = a, b
    dot = functools.partial(
        lax.dot_general, dimension_numbers=(dims, ((), ())), preferred_element_type=F32
    )
    return dot(ah, bh) + (dot(ah, bl) + dot(al, bh))


def kernel(
    n, nh, vis_any, wk_any, wv_any, q_any, g_any, qg_out, kwg_out, vwg_out, vg_out,
    vis, q, g, wk, wv, visf, visl, vist, ql, gl, kvs, kvl, parts, pre, partl, kgs, agl, kgb,
    qgs, qgl, vgp, zz, wst, wx, kgz,
    in_sems, w_sem, q_sems, g_sems, kv_sems, v_sems, vz_sems, pre_sems, part_sems, qg_sems, ag_sems,
    on_sems, z_sems, ws_sems, wz_sems, wx_sems, kz_sems,
):
    me, my_head = lax.axis_index("frame"), lax.axis_index("head")
    rows, depth = vis.shape
    cols = wk.shape[1]
    kv_local = cols // HEAD_DIM
    text_part, width = ql.shape[1], ql.shape[2]
    split = q.shape[0] // text_part
    heads = width // HEAD_DIM
    share = n // kv_local
    dn, dh = depth // n, depth // nh
    chunk = depth // CHUNKS
    tile = dh // TILES
    factor = HEAD_DIM ** (-0.5)
    bounds = [0]
    for u in UNITS:
        bounds.append(bounds[-1] + u * dn // sum(UNITS))
    ahead = [0] + [NEAR] * (nh - 2) + [FAR]

    def frame_copy_of(src, dst, send_sem, recv_sem, target):
        return pltpu.make_async_remote_copy(
            src_ref=src, dst_ref=dst, send_sem=send_sem, recv_sem=recv_sem,
            device_id={"frame": target}, device_id_type=MESH,
        )

    def frame_copy(src, dst, sems, slot_send, slot_recv, target):
        return frame_copy_of(src, dst, sems.at[0, slot_send], sems.at[1, slot_recv], target)

    def head_copy(src, dst, send_sem, recv_sem, target):
        return pltpu.make_async_remote_copy(
            src_ref=src, dst_ref=dst, send_sem=send_sem, recv_sem=recv_sem,
            device_id={"head": target}, device_id_type=MESH,
        )

    def peer(k):
        return lax.rem(me + k, n)

    def source(k):
        return lax.rem(me + n - k, n)

    core, chip, chips = lax.rem(me, 2), me // 2, n // 2
    sibling = me + 1 - 2 * core

    def mate(j):
        return lax.rem(me + 2 * j, n)

    def mate_source(j):
        return lax.rem(me + n - 2 * j, n)

    sends = []

    def send(copy):
        copy.start()
        sends.append(copy)

    def spread(pick, land, sems):
        send(frame_copy(pick(sibling), land.at[me], sems, sibling, me, sibling))
        for j in range(1, chips):
            p = mate(j)
            send(frame_copy(pick(p), land.at[me], sems, p, me, p))

    def forward(land, sems, on):
        for j in range(1, chips):
            s = mate_source(j)
            frame_copy(land.at[s], land.at[s], sems, s, s, s).wait_recv()
            send(frame_copy_of(land.at[s], land.at[s], on.at[s], sems.at[1, s], sibling))

    def wait_rest(land, sems):
        frame_copy(land.at[sibling], land.at[sibling], sems, sibling, sibling, sibling).wait_recv()
        for j in range(1, chips):
            s = lax.rem(sibling + n - 2 * j, n)
            frame_copy(land.at[s], land.at[s], sems, s, s, sibling).wait_recv()

    def wait_all(land, sems):
        for k in range(1, n):
            s = source(k)
            frame_copy(land.at[s], land.at[s], sems, s, s, s).wait_recv()

    def to_vmem(src, dst, sem):
        copy = pltpu.make_async_copy(src, dst, sem)
        copy.start()
        return copy

    texts_in = [to_vmem(q_any, q, in_sems.at[0]), to_vmem(g_any, g, in_sems.at[1])]
    vis_in = to_vmem(vis_any, vis, in_sems.at[2])
    loads = [
        [
            to_vmem(src.at[pl.ds(c * chunk, chunk)], dst.at[pl.ds(c * chunk, chunk)], w_sem.at[i, c])
            for c in range(CHUNKS)
        ]
        for i, (src, dst) in enumerate(((wk_any, wk), (wv_any, wv)))
    ]

    barrier = pltpu.get_barrier_semaphore()
    for k in range(1, n):
        pl.semaphore_signal(barrier, inc=1, device_id={"frame": peer(k)}, device_id_type=MESH)
    for j in range(1, nh):
        pl.semaphore_signal(
            barrier, inc=1, device_id={"head": lax.rem(my_head + j, nh)}, device_id_type=MESH
        )
    pl.semaphore_wait(barrier, n + nh - 2)

    def text_at(p):
        part, block = lax.rem(p, split), p // split
        return (
            pl.ds(pl.multiple_of(part * text_part, text_part), text_part),
            pl.ds(pl.multiple_of(block * width, width), width),
        )

    def send_text(copy, src, dst, sems):
        copy.wait()
        for k in range(1, n):
            p = peer(k)
            send(frame_copy(src.at[text_at(p)], dst.at[me], sems, p, me, p))
        dst[me] = src[text_at(me)]

    def project(i, w):
        acc = jnp.zeros((rows, cols), F32)
        for c in range(CHUNKS):
            if i == 0:
                loads[i][c].wait()
            at = pl.ds(c * chunk, chunk)
            acc += jnp.dot(vis[:, at], w[at], preferred_element_type=F32)
        for a in range(kv_local):
            kvs[i, a] = acc[:, a * HEAD_DIM : (a + 1) * HEAD_DIM]
        spread(lambda p: kvs.at[i, p // share], kvl.at[i], kv_sems.at[i])
        kvl[i, me] = kvs[i, me // share]

    quarter = bounds[1] // nh

    def quarter_at(h):
        return pl.ds(pl.multiple_of(h * quarter, quarter), quarter)

    def onward_head(way):
        return jnp.clip(my_head + 1 - 2 * way, 0, nh - 1)

    def can_go(way):
        return my_head < nh - 1 if way == 0 else my_head > 0

    def quarter_copy(way, s):
        land = visl.at[:, quarter_at(s)]
        return head_copy(land, land, vz_sems.at[0, way, s], vz_sems.at[1, way, s], onward_head(way))

    def turn_visual(i):
        at = slice(bounds[i], bounds[i + 1])
        for p in range(n):
            block = vis[:, p * dn + bounds[i] : p * dn + bounds[i + 1]]
            visf[p, at] = block.astype(F32).T
        if i > 0:
            visl[me, at] = visf[me, at]

    def share_visual():
        at = quarter_at(my_head)
        visl[me, at] = visf[me, at]
        for k in range(1, n):
            p = peer(k)
            send(frame_copy(visf.at[p, at], visl.at[me, at], v_sems.at[0], p, me, p))

    def pass_visual():
        at = quarter_at(my_head)
        for k in range(1, n):
            s = source(k)
            frame_copy(visl.at[s, at], visl.at[s, at], v_sems.at[0], s, s, s).wait_recv()
        for way in range(2):

            @pl.when(can_go(way))
            def _():
                quarter_copy(way, my_head).start()

    def relay_visual(j):
        for way in range(2):
            s = my_head - j if way == 0 else my_head + j

            @pl.when(jnp.logical_and(s >= 0, s < nh))
            def _():
                quarter_copy(way, jnp.clip(s, 0, nh - 1)).wait_recv()

                @pl.when(can_go(way))
                def _():
                    quarter_copy(way, jnp.clip(s, 0, nh - 1)).start()

    def send_visual(i):
        at = pl.ds(bounds[i], bounds[i + 1] - bounds[i])
        for k in range(1, n):
            p = peer(k)
            send(frame_copy(visf.at[p, at], visl.at[me, at], v_sems.at[i], p, me, p))

    def take_visual(i):
        at = pl.ds(bounds[i], bounds[i + 1] - bounds[i])
        if i > 0:
            for k in range(1, n):
                s = source(k)
                land = visl.at[s, at]
                frame_copy(land, land, v_sems.at[i], s, s, s).wait_recv()
        for s in range(n):
            vist[at, s * rows : (s + 1) * rows] = visl[s, at].astype(BF16)
        for j, out in enumerate((kwg_out, vwg_out)):
            out[at] = jnp.dot(vist[at], kgb[j], preferred_element_type=F32)

    is_end = jnp.logical_or(my_head == 0, my_head == nh - 1)
    staged = [(t, c) for t in range(nh - 1, 0, -1) for c in range(ahead[t])]
    slots = wx.shape[1]
    tw = tile // n

    def slot_of(t, c):
        return c if t == nh - 1 else jnp.where(my_head == 0, c, NEAR + c)

    def stage_copy(k):
        t, c = staged[k]
        d = jnp.where(my_head == 0, t, nh - 1 - t)
        return head_copy(
            wst.at[k], wx.at[me, slot_of(t, c)], ws_sems.at[k], wz_sems.at[slot_of(t, c)], d
        )

    send_text(texts_in[0], q, ql, q_sems)
    vis_in.wait()
    turn_visual(0)
    project(0, wk)
    for c in range(CHUNKS):
        loads[1][c].wait()
    if staged:

        @pl.when(is_end)
        def _():
            for k, (t, c) in enumerate(staged):
                d = jnp.where(my_head == 0, t, nh - 1 - t)
                at = pl.ds(pl.multiple_of(d * dh + c * tile + me * tw, tw), tw)
                for i, w in enumerate((wk, wv)):
                    wst[k, i] = w[at].astype(F32)
                stage_copy(k).start()

    send_text(texts_in[1], g, gl, g_sems)
    share_visual()
    project(1, wv)

    turn_visual(1)
    send_visual(1)
    for i in range(2, len(UNITS)):
        turn_visual(i)

    forward(kvl.at[0], kv_sems.at[0], on_sems.at[0])
    wait_all(ql, q_sems)
    wait_rest(kvl.at[0], kv_sems.at[0])
    keys = kvl[0].reshape(n * rows, HEAD_DIM)
    texts = [slice(h * HEAD_DIM, (h + 1) * HEAD_DIM) for h in range(heads)]
    queries = [ql[:, :, at].reshape(n * text_part, HEAD_DIM) for at in texts]
    probs = []
    for query in queries:
        scores = lax.dot_general(
            keys, query, LANES, precision=lax.Precision.HIGHEST, preferred_element_type=F32
        ) * factor
        raw = jnp.exp(scores - jnp.max(scores, axis=0, keepdims=True))
        probs.append(raw * (1.0 / jnp.sum(raw, axis=0, keepdims=True)))

    pass_visual()
    forward(kvl.at[1], kv_sems.at[1], on_sems.at[1])
    wait_all(gl, g_sems)
    grads2 = [halves(gl[:, :, at].reshape(n * text_part, HEAD_DIM)) for at in texts]

    def gather_ahead():
        for j in range(slots):
            land = wx.at[me, j]
            head_copy(land, land, wz_sems.at[j], wz_sems.at[j], my_head).wait_recv()
        spread(lambda p: wx.at[me], wx, wx_sems)

    def total(terms):
        out = terms[0]
        for term in terms[1:]:
            out = out + term
        return out

    def exchange(i):
        return frame_copy_of(
            parts.at[i, 1 - core], pre.at[i], pre_sems.at[i, 0], pre_sems.at[i, 1], sibling
        )

    def give(i, part):
        part = part.reshape(chips, 2, rows, HEAD_DIM)
        for c in range(2):
            parts[i, c] = part[:, c]
        send(exchange(i))

    def pass_on(i):
        exchange(i).wait_recv()
        parts[i, core] += pre[i]
        for j in range(1, chips):
            p = mate(j)
            send(
                frame_copy(
                    parts.at[i, core, p // 2], partl.at[i, chip], part_sems.at[i], p // 2, chip, p
                )
            )
        partl[i, chip] = parts[i, core, chip]

    give(1, total([product(halves(p), g2, ((1,), (0,))) for p, g2 in zip(probs, grads2)]))

    wait_rest(kvl.at[1], kv_sems.at[1])
    values2 = halves(kvl[1].reshape(n * rows, HEAD_DIM))
    dscores2 = []
    for h, (p, g2) in enumerate(zip(probs, grads2)):
        dprob = product(values2, g2, ((1,), (1,)))
        delta = jnp.sum(p * dprob, axis=0, keepdims=True)
        dscores2.append(halves(p * (dprob - delta)))
        if h == 0:
            pass_on(1)
    give(0, total([product(d2, halves(query), ((1,), (0,))) for d2, query in zip(dscores2, queries)]))
    keys_t = halves(keys.T)
    for d2, at in zip(dscores2, texts):
        query_term = product(keys_t, d2, ((1,), (0,))).T * factor
        qgs[:, :, at] = query_term.reshape(n, text_part, HEAD_DIM)
    pass_on(0)
    relay_visual(1)
    if staged:
        gather_ahead()
    send_visual(2)

    low = [None, None]
    for i in (1, 0):
        for j in range(1, chips):
            s = mate_source(j)
            land = partl.at[i, s // 2]
            frame_copy(land, land, part_sems.at[i], s // 2, s // 2, s).wait_recv()
        for a in range(kv_local):
            column = total([partl[i, p] for p in range(a * share // 2, (a + 1) * share // 2)])
            if i == 0:
                column = column * factor
            kgs[i, :, a * HEAD_DIM : (a + 1) * HEAD_DIM] = column.astype(BF16).astype(F32)
        low[i] = kgs[i].astype(BF16)

    lead = jnp.where(2 * my_head < nh, 0, 1)

    def block_of(way, t):
        return jnp.where(way == 0, t, nh - 1 - t)

    def rank(way):
        return jnp.where(way == 0, my_head, nh - 1 - my_head)

    def visual_term(d, c):
        at = pl.ds(pl.multiple_of(d * dh + c * tile, tile), tile)
        vgp[d, c] = lax.dot_general(
            low[0], wk[at], LANES, preferred_element_type=F32
        ) + lax.dot_general(low[1], wv[at], LANES, preferred_element_type=F32)

    def hop(way, d, c):
        return head_copy(
            vgp.at[d, c], zz.at[way, d, c], z_sems.at[way, 0, d, c], z_sems.at[way, 1, d, c],
            onward_head(way),
        )

    def starts(t, c):
        return 1 if c < ahead[t] else 0

    def relay(way, t, c):
        d, first = block_of(way, t), starts(t, c)

        @pl.when(jnp.logical_and(rank(way) < t, rank(way) >= first))
        def _():
            @pl.when(rank(way) > first)
            def _():
                hop(way, d, c).wait_recv()
                vgp[d, c] += zz[way, d, c]

            hop(way, d, c).start()

    def kg_hop(way, first):
        return head_copy(
            kgs if first else kgz.at[way], kgz.at[way], kz_sems.at[way, 0], kz_sems.at[way, 1],
            onward_head(way),
        )

    def relay_grads(way):
        @pl.when(rank(way) == 0)
        def _():
            kg_hop(way, True).start()

        @pl.when(jnp.logical_and(rank(way) > 0, rank(way) < nh - 1))
        def _():
            kg_hop(way, False).wait_recv()
            kg_hop(way, False).start()

    def add_ahead():
        for way in range(2):

            @pl.when(rank(way) == nh - 1)
            def _():
                kg_hop(way, False).wait_recv()

        wait_rest(wx, wx_sems)
        for j in range(slots):
            from_right = jnp.where(is_end, jnp.where(my_head == 0, 1, 0), 1 if j >= NEAR else 0)
            c = jnp.where(is_end, j, j % NEAR)
            term = vgp[my_head, c]
            for i in range(2):
                block = wx[:, j, i].reshape(tile, cols).astype(BF16)
                term += lax.dot_general(
                    kgz[from_right, i].astype(BF16), block, LANES, preferred_element_type=F32
                )
            vgp[my_head, c] = term

    spread(lambda p: kgs, agl, ag_sems)
    agl[me] = kgs[...]
    for k in range(1, n):
        p = peer(k)
        send(frame_copy(qgs.at[p], qgl.at[me], qg_sems, p, me, p))
    qgl[me] = qgs[me]
    for i in range(3, len(UNITS)):
        send_visual(i)

    order = [(t, c) for t in range(nh - 1, 0, -1) for c in range(TILES)]

    def visual_terms(way, t, c):
        @pl.when(rank(way) >= starts(t, c))
        def _():
            visual_term(block_of(way, t), c)

    for k in range(len(order) + LAG):
        if k < len(order):
            t, c = order[k]
            if 2 * t > nh - 1:
                visual_terms(lead, t, c)
                visual_terms(1 - lead, t, c)
            if k == FAR:
                if staged:
                    relay_grads(lead)
            relay(lead, t, c)
        if k >= LAG:
            if k - LAG == TILES and staged:
                relay_grads(1 - lead)
            relay(1 - lead, *order[k - LAG])
        if k == 2 and nh > 2:
            relay_visual(2)

    for j in range(3, nh):
        relay_visual(j)
    forward(agl, ag_sems, on_sems.at[2])
    if staged:
        forward(wx, wx_sems, on_sems.at[3])
    wait_rest(agl, ag_sems)
    for i in range(2):
        kgb[i] = agl[:, i].reshape(n * rows, cols).astype(BF16)
    for i in range(3):
        take_visual(i)
    wait_all(qgl, qg_sems)
    for s in range(n):
        part, block = s % split, s // split
        qg_out[
            part * text_part : (part + 1) * text_part, block * width : (block + 1) * width
        ] = qgl[s]
    if staged:
        add_ahead()
    for i in range(3, len(UNITS)):
        take_visual(i)

    for c in range(TILES):
        at = slice(c * tile, (c + 1) * tile)
        vg_out[:, at] = vgp[my_head, c]
        for way in (lead, 1 - lead):
            t = rank(way)
            count = jnp.where(t == nh - 1, FAR, NEAR)

            @pl.when(t > jnp.where(c < count, 1, 0))
            def _():
                hop(way, my_head, c).wait_recv()
                vg_out[:, at] += zz[way, my_head, c]

    for way in (lead, 1 - lead):
        for t, c in order:

            @pl.when(jnp.logical_and(rank(way) < t, rank(way) >= starts(t, c)))
            def _():
                hop(way, block_of(way, t), c).wait_send()

        if staged:

            @pl.when(rank(way) < nh - 1)
            def _():
                kg_hop(way, True).wait_send()

    if staged:

        @pl.when(is_end)
        def _():
            for k in range(len(staged)):
                stage_copy(k).wait_send()

    for way in range(2):
        for j in range(nh):
            s = my_head - j if way == 0 else my_head + j

            @pl.when(jnp.logical_and(jnp.logical_and(s >= 0, s < nh), can_go(way)))
            def _():
                quarter_copy(way, jnp.clip(s, 0, nh - 1)).wait_send()

    for copy in sends:
        copy.wait_send()


def store(*refs):
    outs, sems = refs[len(refs) // 2 : -1], refs[-1]
    copies = [
        pltpu.make_async_copy(src, dst, sems.at[i]) for i, (src, dst) in enumerate(zip(refs, outs))
    ]
    for copy in copies:
        copy.start()
    for copy in copies:
        copy.wait()


def solution(mesh):
    n, nh = mesh.shape["frame"], mesh.shape["head"]

    def body(visual, w_key, w_value, queries, out_grad):
        rows, depth = visual.shape
        cols = w_key.shape[1]
        text, query_cols = queries.shape
        local_heads = query_cols // HEAD_DIM
        split = max(1, n // local_heads)
        part, width = text // split, query_cols * split // n
        vmem = pl.BlockSpec(memory_space=pltpu.VMEM)
        hbm = pl.BlockSpec(memory_space=pl.ANY)
        dn, dh = depth // n, depth // nh
        tile = dh // TILES
        slots = max(FAR, 2 * NEAR, 1)
        pairs = pltpu.SemaphoreType.DMA((2, n))
        dma = pltpu.SemaphoreType.DMA
        outs = pl.pallas_call(
            functools.partial(kernel, n, nh),
            out_shape=(
                pltpu.VMEM((text, query_cols), F32),
                pltpu.VMEM((dn, cols), F32),
                pltpu.VMEM((dn, cols), F32),
                pltpu.VMEM((rows, dh), F32),
            ),
            in_specs=[hbm] * 5,
            out_specs=(vmem,) * 4,
            scratch_shapes=[
                pltpu.VMEM((rows, depth), BF16),
                pltpu.VMEM((text, query_cols), F32),
                pltpu.VMEM((text, query_cols), F32),
                pltpu.VMEM((depth, cols), BF16),
                pltpu.VMEM((depth, cols), BF16),
                pltpu.VMEM((n, dn, rows), F32),
                pltpu.VMEM((n, dn, rows), F32),
                pltpu.VMEM((dn, n * rows), BF16),
                pltpu.VMEM((n, part, width), F32),
                pltpu.VMEM((n, part, width), F32),
                pltpu.VMEM((2, cols // HEAD_DIM, rows, HEAD_DIM), F32),
                pltpu.VMEM((2, n, rows, HEAD_DIM), F32),
                pltpu.VMEM((2, 2, n // 2, rows, HEAD_DIM), F32),
                pltpu.VMEM((2, n // 2, rows, HEAD_DIM), F32),
                pltpu.VMEM((2, n // 2, rows, HEAD_DIM), F32),
                pltpu.VMEM((2, rows, cols), F32),
                pltpu.VMEM((n, 2, rows, cols), F32),
                pltpu.VMEM((2, n * rows, cols), BF16),
                pltpu.VMEM((n, part, width), F32),
                pltpu.VMEM((n, part, width), F32),
                pltpu.VMEM((nh, TILES, rows, tile), F32),
                pltpu.VMEM((2, nh, TILES, rows, tile), F32),
                pltpu.VMEM((max(FAR + NEAR * (nh - 2), 1), 2, tile // n, cols), F32),
                pltpu.VMEM((n, slots, 2, tile // n, cols), F32),
                pltpu.VMEM((2, 2, rows, cols), F32),
                dma((3,)),
                dma((2, CHUNKS)),
                pairs, pairs,
                dma((2, 2, n)),
                dma((len(UNITS), 2, n)),
                dma((2, 2, nh)),
                dma((2, 2)),
                dma((2, 2, n // 2)),
                pairs, pairs,
                dma((4, n)),
                dma((2, 2, nh, TILES)),
                dma((max(FAR + NEAR * (nh - 2), 1),)),
                dma((slots,)),
                pairs,
                dma((2, 2)),
            ],
            compiler_params=pltpu.CompilerParams(
                collective_id=0, has_side_effects=True, vmem_limit_bytes=60000000
            ),
        )(visual, w_key, w_value, queries, out_grad)
        return pl.pallas_call(
            store,
            out_shape=tuple(jax.ShapeDtypeStruct(o.shape, o.dtype) for o in outs),
            in_specs=[vmem] * 4,
            out_specs=(hbm,) * 4,
            scratch_shapes=[dma((4,))],
            compiler_params=pltpu.CompilerParams(vmem_limit_bytes=1 << 20),
        )(*[pltpu.with_memory_space_constraint(o, pltpu.VMEM) for o in outs])

    return jax.shard_map(
        body,
        mesh=mesh,
        in_specs=(
            P("frame", None),
            P(None, "head"),
            P(None, "head"),
            P("frame", "head"),
            P("frame", "head"),
        ),
        out_specs=(P("frame", "head"), P("frame", "head"), P("frame", "head"), P("frame", "head")),
        check_vma=False,
    )
```

```python
import functools

import jax
import jax.numpy as jnp
from jax import lax
from jax.experimental import pallas as pl
from jax.experimental.pallas import tpu as pltpu
from jax.sharding import PartitionSpec as P

HEAD_DIM = 128
MESH = pl.DeviceIdType.MESH
CHUNKS = 8
TILES = 8
UNITS = (1, 1, 2, 2, 2)
FAR, NEAR = 4, 2
LAG = 3
F32, BF16 = jnp.float32, jnp.bfloat16
LANES = (((1,), (1,)), ((), ()))


def halves(a):
    high = a.astype(BF16)
    return high, (a - high.astype(F32)).astype(BF16)


def product(a, b, dims):
    (ah, al), (bh, bl) = a, b
    dot = functools.partial(
        lax.dot_general, dimension_numbers=(dims, ((), ())), preferred_element_type=F32
    )
    return dot(ah, bh) + (dot(ah, bl) + dot(al, bh))


def kernel(
    n, nh, vis_any, wk_any, wv_any, q_any, g_any, qg_out, kwg_out, vwg_out, vg_out,
    vis, q, g, wk, wv, visf, visl, vist, ql, gl, kvs, kvl, parts, pre, partl, kgs, agl, kgb,
    qgs, qgl, vgp, zz, wst, wx, kgz,
    in_sems, w_sem, q_sems, g_sems, kv_sems, v_sems, vz_sems, pre_sems, part_sems, qg_sems, ag_sems,
    on_sems, z_sems, ws_sems, wz_sems, wx_sems, kz_sems,
):
    me, my_head = lax.axis_index("frame"), lax.axis_index("head")
    rows, depth = vis.shape
    cols = wk.shape[1]
    kv_local = cols // HEAD_DIM
    text_part, width = ql.shape[1], ql.shape[2]
    split = q.shape[0] // text_part
    heads = width // HEAD_DIM
    share = n // kv_local
    dn, dh = depth // n, depth // nh
    chunk = depth // CHUNKS
    tile = dh // TILES
    factor = HEAD_DIM ** (-0.5)
    bounds = [0]
    for u in UNITS:
        bounds.append(bounds[-1] + u * dn // sum(UNITS))
    ahead = [0] + [NEAR] * (nh - 2) + [FAR]

    def frame_copy_of(src, dst, send_sem, recv_sem, target):
        return pltpu.make_async_remote_copy(
            src_ref=src, dst_ref=dst, send_sem=send_sem, recv_sem=recv_sem,
            device_id={"frame": target}, device_id_type=MESH,
        )

    def frame_copy(src, dst, sems, slot_send, slot_recv, target):
        return frame_copy_of(src, dst, sems.at[0, slot_send], sems.at[1, slot_recv], target)

    def head_copy(src, dst, send_sem, recv_sem, target):
        return pltpu.make_async_remote_copy(
            src_ref=src, dst_ref=dst, send_sem=send_sem, recv_sem=recv_sem,
            device_id={"head": target}, device_id_type=MESH,
        )

    def peer(k):
        return lax.rem(me + k, n)

    def source(k):
        return lax.rem(me + n - k, n)

    core, chip, chips = lax.rem(me, 2), me // 2, n // 2
    sibling = me + 1 - 2 * core

    def mate(j):
        return lax.rem(me + 2 * j, n)

    def mate_source(j):
        return lax.rem(me + n - 2 * j, n)

    sends, late = [], []

    def send(copy, kept=sends):
        copy.start()
        kept.append(copy)

    def spread(pick, land, sems):
        send(frame_copy(pick(sibling), land.at[me], sems, sibling, me, sibling))
        for j in range(1, chips):
            p = mate(j)
            send(frame_copy(pick(p), land.at[me], sems, p, me, p))

    def forward(land, sems, on):
        for j in range(1, chips):
            s = mate_source(j)
            frame_copy(land.at[s], land.at[s], sems, s, s, s).wait_recv()
            send(frame_copy_of(land.at[s], land.at[s], on.at[s], sems.at[1, s], sibling))

    def wait_rest(land, sems):
        frame_copy(land.at[sibling], land.at[sibling], sems, sibling, sibling, sibling).wait_recv()
        for j in range(1, chips):
            s = lax.rem(sibling + n - 2 * j, n)
            frame_copy(land.at[s], land.at[s], sems, s, s, sibling).wait_recv()

    def wait_all(land, sems):
        for k in range(1, n):
            s = source(k)
            frame_copy(land.at[s], land.at[s], sems, s, s, s).wait_recv()

    def to_vmem(src, dst, sem):
        copy = pltpu.make_async_copy(src, dst, sem)
        copy.start()
        return copy

    texts_in = [to_vmem(q_any, q, in_sems.at[0]), to_vmem(g_any, g, in_sems.at[1])]
    vis_in = to_vmem(vis_any, vis, in_sems.at[2])
    loads = [
        [
            to_vmem(src.at[pl.ds(c * chunk, chunk)], dst.at[pl.ds(c * chunk, chunk)], w_sem.at[i, c])
            for c in range(CHUNKS)
        ]
        for i, (src, dst) in enumerate(((wk_any, wk), (wv_any, wv)))
    ]

    barrier = pltpu.get_barrier_semaphore()
    for k in range(1, n):
        pl.semaphore_signal(barrier, inc=1, device_id={"frame": peer(k)}, device_id_type=MESH)
    for j in range(1, nh):
        pl.semaphore_signal(
            barrier, inc=1, device_id={"head": lax.rem(my_head + j, nh)}, device_id_type=MESH
        )
    pl.semaphore_wait(barrier, n + nh - 2)

    def text_at(p):
        part, block = lax.rem(p, split), p // split
        return (
            pl.ds(pl.multiple_of(part * text_part, text_part), text_part),
            pl.ds(pl.multiple_of(block * width, width), width),
        )

    def send_text(copy, src, dst, sems):
        copy.wait()
        for k in range(1, n):
            p = peer(k)
            send(frame_copy(src.at[text_at(p)], dst.at[me], sems, p, me, p))
        dst[me] = src[text_at(me)]

    def project(i, w):
        acc = jnp.zeros((rows, cols), F32)
        for c in range(CHUNKS):
            if i == 0:
                loads[i][c].wait()
            at = pl.ds(c * chunk, chunk)
            acc += jnp.dot(vis[:, at], w[at], preferred_element_type=F32)
        for a in range(kv_local):
            kvs[i, a] = acc[:, a * HEAD_DIM : (a + 1) * HEAD_DIM]
        spread(lambda p: kvs.at[i, p // share], kvl.at[i], kv_sems.at[i])
        kvl[i, me] = kvs[i, me // share]

    quarter = bounds[1] // nh

    def quarter_at(h):
        return pl.ds(pl.multiple_of(h * quarter, quarter), quarter)

    def onward_head(way):
        return jnp.clip(my_head + 1 - 2 * way, 0, nh - 1)

    def can_go(way):
        return my_head < nh - 1 if way == 0 else my_head > 0

    def quarter_copy(way, s):
        land = visl.at[:, quarter_at(s)]
        return head_copy(land, land, vz_sems.at[0, way, s], vz_sems.at[1, way, s], onward_head(way))

    def turn_visual(i):
        at = slice(bounds[i], bounds[i + 1])
        for p in range(n):
            block = vis[:, p * dn + bounds[i] : p * dn + bounds[i + 1]]
            visf[p, at] = block.astype(F32).T
        if i > 0:
            visl[me, at] = visf[me, at]

    def share_visual():
        at = quarter_at(my_head)
        visl[me, at] = visf[me, at]
        for k in range(1, n):
            p = peer(k)
            send(frame_copy(visf.at[p, at], visl.at[me, at], v_sems.at[0], p, me, p))

    def pass_visual():
        at = quarter_at(my_head)
        for k in range(1, n):
            s = source(k)
            frame_copy(visl.at[s, at], visl.at[s, at], v_sems.at[0], s, s, s).wait_recv()
        for way in range(2):

            @pl.when(can_go(way))
            def _():
                quarter_copy(way, my_head).start()

    def relay_visual(j):
        for way in range(2):
            s = my_head - j if way == 0 else my_head + j

            @pl.when(jnp.logical_and(s >= 0, s < nh))
            def _():
                quarter_copy(way, jnp.clip(s, 0, nh - 1)).wait_recv()

                @pl.when(can_go(way))
                def _():
                    quarter_copy(way, jnp.clip(s, 0, nh - 1)).start()

    def send_visual(i):
        at = pl.ds(bounds[i], bounds[i + 1] - bounds[i])
        kept = late if i == len(UNITS) - 1 else sends
        for k in range(1, n):
            p = peer(k)
            send(frame_copy(visf.at[p, at], visl.at[me, at], v_sems.at[i], p, me, p), kept)

    def take_visual(i):
        at = pl.ds(bounds[i], bounds[i + 1] - bounds[i])
        if i > 0:
            for k in range(1, n):
                s = source(k)
                land = visl.at[s, at]
                frame_copy(land, land, v_sems.at[i], s, s, s).wait_recv()
        for s in range(n):
            vist[at, s * rows : (s + 1) * rows] = visl[s, at].astype(BF16)
        for j, out in enumerate((kwg_out, vwg_out)):
            out[at] = jnp.dot(vist[at], kgb[j], preferred_element_type=F32)

    is_end = jnp.logical_or(my_head == 0, my_head == nh - 1)
    staged = [(t, c) for t in range(nh - 1, 0, -1) for c in range(ahead[t])]
    slots = wx.shape[1]
    tw = tile // n

    def slot_of(t, c):
        return c if t == nh - 1 else jnp.where(my_head == 0, c, NEAR + c)

    square = chips == 4
    far_core = 6 - 2 * chip + core
    direct = (me, far_core) if square else (me,)

    def stage_copy(k, b):
        t, c = staged[k]
        d = jnp.where(my_head == 0, t, nh - 1 - t)
        return head_copy(
            wst.at[k, b], wx.at[direct[b], slot_of(t, c)], ws_sems.at[k, b],
            wz_sems.at[b, slot_of(t, c)], d,
        )

    send_text(texts_in[0], q, ql, q_sems)
    vis_in.wait()
    turn_visual(0)
    project(0, wk)
    for c in range(CHUNKS):
        loads[1][c].wait()
    if staged:

        @pl.when(is_end)
        def _():
            for k, (t, c) in enumerate(staged):
                d = jnp.where(my_head == 0, t, nh - 1 - t)
                for b, owner in enumerate(direct):
                    at = pl.ds(pl.multiple_of(d * dh + c * tile + owner * tw, tw), tw)
                    for i, w in enumerate((wk, wv)):
                        wst[k, b, i] = w[at].astype(F32)
                    stage_copy(k, b).start()

    send_text(texts_in[1], g, gl, g_sems)
    project(1, wv)
    share_visual()

    turn_visual(1)
    send_visual(1)
    for i in range(2, len(UNITS)):
        turn_visual(i)

    forward(kvl.at[0], kv_sems.at[0], on_sems.at[0])
    wait_all(ql, q_sems)
    wait_rest(kvl.at[0], kv_sems.at[0])
    keys = kvl[0].reshape(n * rows, HEAD_DIM)
    texts = [slice(h * HEAD_DIM, (h + 1) * HEAD_DIM) for h in range(heads)]
    queries = [ql[:, :, at].reshape(n * text_part, HEAD_DIM) for at in texts]
    probs = []
    for query in queries:
        scores = lax.dot_general(
            keys, query, LANES, precision=lax.Precision.HIGHEST, preferred_element_type=F32
        ) * factor
        raw = jnp.exp(scores - jnp.max(scores, axis=0, keepdims=True))
        probs.append(raw * (1.0 / jnp.sum(raw, axis=0, keepdims=True)))

    forward(kvl.at[1], kv_sems.at[1], on_sems.at[1])
    wait_all(gl, g_sems)
    grads2 = [halves(gl[:, :, at].reshape(n * text_part, HEAD_DIM)) for at in texts]

    def gather_ahead():
        for b, owner in enumerate(direct):
            for j in range(slots):
                land = wx.at[owner, j]
                head_copy(land, land, wz_sems.at[b, j], wz_sems.at[b, j], my_head).wait_recv()
        if square:
            for p in near_mates(me) + [sibling]:
                send(frame_copy(wx.at[me], wx.at[me], wx_sems, p, me, p))
            send(frame_copy_of(wx.at[far_core], wx.at[far_core], on_sems.at[3, far_core], wx_sems.at[1, far_core], sibling))
        else:
            spread(lambda p: wx.at[me], wx, wx_sems)

    def near_mates(d):
        c, b = d // 2, lax.rem(d, 2)
        return [2 * (c + 1 - 2 * lax.rem(c, 2)) + b, 2 * lax.rem(c + 2, 4) + b]

    def forward_ahead():
        if not square:
            forward(wx, wx_sems, on_sems.at[3])
            wait_rest(wx, wx_sems)
            return
        for s in near_mates(me):
            frame_copy(wx.at[s], wx.at[s], wx_sems, s, s, s).wait_recv()
            send(frame_copy_of(wx.at[s], wx.at[s], on_sems.at[3, s], wx_sems.at[1, s], sibling))

    def rest_ahead():
        if square:
            for s in near_mates(sibling) + [sibling, far_core + 1 - 2 * core]:
                frame_copy(wx.at[s], wx.at[s], wx_sems, s, s, sibling).wait_recv()

    def total(terms):
        out = terms[0]
        for term in terms[1:]:
            out = out + term
        return out

    def exchange(i):
        return frame_copy_of(
            parts.at[i, 1 - core], pre.at[i], pre_sems.at[i, 0], pre_sems.at[i, 1], sibling
        )

    def give(i, part):
        part = part.reshape(chips, 2, rows, HEAD_DIM)
        for c in range(2):
            parts[i, c] = part[:, c]
        send(exchange(i))

    def pass_on(i):
        exchange(i).wait_recv()
        parts[i, core] += pre[i]
        for j in range(1, chips):
            p = mate(j)
            send(
                frame_copy(
                    parts.at[i, core, p // 2], partl.at[i, chip], part_sems.at[i], p // 2, chip, p
                )
            )
        partl[i, chip] = parts[i, core, chip]

    give(1, total([product(halves(p), g2, ((1,), (0,))) for p, g2 in zip(probs, grads2)]))

    wait_rest(kvl.at[1], kv_sems.at[1])
    values2 = halves(kvl[1].reshape(n * rows, HEAD_DIM))
    dscores2 = []
    for h, (p, g2) in enumerate(zip(probs, grads2)):
        dprob = product(values2, g2, ((1,), (1,)))
        delta = jnp.sum(p * dprob, axis=0, keepdims=True)
        dscores2.append(halves(p * (dprob - delta)))
        if h == 0:
            pass_on(1)
    give(0, total([product(d2, halves(query), ((1,), (0,))) for d2, query in zip(dscores2, queries)]))
    pass_visual()
    keys_t = halves(keys.T)
    for d2, at in zip(dscores2, texts):
        query_term = product(keys_t, d2, ((1,), (0,))).T * factor
        qgs[:, :, at] = query_term.reshape(n, text_part, HEAD_DIM)
    pass_on(0)
    if staged:
        gather_ahead()
    send_visual(2)

    low = [None, None]
    for i in (1, 0):
        for j in range(1, chips):
            s = mate_source(j)
            land = partl.at[i, s // 2]
            frame_copy(land, land, part_sems.at[i], s // 2, s // 2, s).wait_recv()
        for a in range(kv_local):
            column = total([partl[i, p] for p in range(a * share // 2, (a + 1) * share // 2)])
            if i == 0:
                column = column * factor
            kgs[i, :, a * HEAD_DIM : (a + 1) * HEAD_DIM] = column.astype(BF16).astype(F32)
        low[i] = kgs[i].astype(BF16)

    lead = jnp.where(2 * my_head < nh, 0, 1)

    def block_of(way, t):
        return jnp.where(way == 0, t, nh - 1 - t)

    def rank(way):
        return jnp.where(way == 0, my_head, nh - 1 - my_head)

    def visual_term(d, c):
        at = pl.ds(pl.multiple_of(d * dh + c * tile, tile), tile)
        vgp[d, c] = lax.dot_general(
            low[0], wk[at], LANES, preferred_element_type=F32
        ) + lax.dot_general(low[1], wv[at], LANES, preferred_element_type=F32)

    def hop(way, d, c):
        return head_copy(
            vgp.at[d, c], zz.at[way, d, c], z_sems.at[way, 0, d, c], z_sems.at[way, 1, d, c],
            onward_head(way),
        )

    def starts(t, c):
        return 1 if c < ahead[t] else 0

    def relay(way, t, c):
        d, first = block_of(way, t), starts(t, c)

        @pl.when(jnp.logical_and(rank(way) < t, rank(way) >= first))
        def _():
            @pl.when(rank(way) > first)
            def _():
                hop(way, d, c).wait_recv()
                vgp[d, c] += zz[way, d, c]

            hop(way, d, c).start()

    def kg_hop(way, first):
        return head_copy(
            kgs if first else kgz.at[way], kgz.at[way], kz_sems.at[way, 0], kz_sems.at[way, 1],
            onward_head(way),
        )

    def start_grads(way):
        @pl.when(rank(way) == 0)
        def _():
            kg_hop(way, True).start()

    def relay_grads(way):
        @pl.when(jnp.logical_and(rank(way) > 0, rank(way) < nh - 1))
        def _():
            kg_hop(way, False).wait_recv()
            kg_hop(way, False).start()

    def add_ahead():
        for way in range(2):

            @pl.when(rank(way) == nh - 1)
            def _():
                kg_hop(way, False).wait_recv()

        rest_ahead()
        for j in range(slots):
            from_right = jnp.where(is_end, jnp.where(my_head == 0, 1, 0), 1 if j >= NEAR else 0)
            c = jnp.where(is_end, j, j % NEAR)
            term = vgp[my_head, c]
            for i in range(2):
                block = wx[:, j, i].reshape(tile, cols).astype(BF16)
                term += lax.dot_general(
                    kgz[from_right, i].astype(BF16), block, LANES, preferred_element_type=F32
                )
            vgp[my_head, c] = term

    def send_rows():
        spread(lambda p: kgs, agl, ag_sems)
        agl[me] = kgs[...]
        for k in range(1, n):
            p = peer(k)
            send(frame_copy(qgs.at[p], qgl.at[me], qg_sems, p, me, p))
        qgl[me] = qgs[me]
        for i in range(3, len(UNITS)):
            send_visual(i)

    order = [(t, c) for t in range(nh - 1, 0, -1) for c in range(TILES)]

    def visual_terms(way, t, c):
        @pl.when(rank(way) >= starts(t, c))
        def _():
            visual_term(block_of(way, t), c)

    if staged:
        start_grads(lead)
    for k in range(len(order) + LAG):
        if k < len(order):
            t, c = order[k]
            if 2 * t > nh - 1:
                visual_terms(lead, t, c)
                visual_terms(1 - lead, t, c)
            if k == FAR:
                if staged:
                    relay_grads(lead)
            relay(lead, t, c)
        if k >= LAG:
            if k - LAG == TILES and staged:
                relay_grads(1 - lead)
            relay(1 - lead, *order[k - LAG])
        if k == FAR - 1:
            send_rows()
        if k == FAR:
            relay_visual(1)
        if k == TILES + 2 and nh > 2:
            relay_visual(2)

    def wait_hops(some):
        for way in (lead, 1 - lead):
            for t, c in some:

                @pl.when(jnp.logical_and(rank(way) < t, rank(way) >= starts(t, c)))
                def _():
                    hop(way, block_of(way, t), c).wait_send()

    for j in range(3, nh):
        relay_visual(j)
    forward(agl, ag_sems, on_sems.at[2])
    if staged:
        forward_ahead()
    wait_rest(agl, ag_sems)
    for i in range(2):
        kgb[i] = agl[:, i].reshape(n * rows, cols).astype(BF16)
    for i in range(3):
        take_visual(i)
    wait_all(qgl, qg_sems)
    for s in range(n):
        part, block = s % split, s // split
        qg_out[
            part * text_part : (part + 1) * text_part, block * width : (block + 1) * width
        ] = qgl[s]
    if staged:
        add_ahead()
    for i in range(3, len(UNITS) - 1):
        take_visual(i)
    for copy in sends:
        copy.wait_send()
    wait_hops(order[: 2 * TILES])
    take_visual(len(UNITS) - 1)

    for c in range(TILES):
        at = slice(c * tile, (c + 1) * tile)
        vg_out[:, at] = vgp[my_head, c]
        for way in (lead, 1 - lead):
            t = rank(way)
            count = jnp.where(t == nh - 1, FAR, NEAR)

            @pl.when(t > jnp.where(c < count, 1, 0))
            def _():
                hop(way, my_head, c).wait_recv()
                vg_out[:, at] += zz[way, my_head, c]

    wait_hops(order[2 * TILES :])
    for way in (lead, 1 - lead):
        if staged:

            @pl.when(rank(way) < nh - 1)
            def _():
                kg_hop(way, True).wait_send()

    if staged:

        @pl.when(is_end)
        def _():
            for k in range(len(staged)):
                for b in range(len(direct)):
                    stage_copy(k, b).wait_send()

    for way in range(2):
        for j in range(nh):
            s = my_head - j if way == 0 else my_head + j

            @pl.when(jnp.logical_and(jnp.logical_and(s >= 0, s < nh), can_go(way)))
            def _():
                quarter_copy(way, jnp.clip(s, 0, nh - 1)).wait_send()

    for copy in late:
        copy.wait_send()


def store(*refs):
    outs, sems = refs[len(refs) // 2 : -1], refs[-1]
    copies = [
        pltpu.make_async_copy(src, dst, sems.at[i]) for i, (src, dst) in enumerate(zip(refs, outs))
    ]
    for copy in copies:
        copy.start()
    for copy in copies:
        copy.wait()


def solution(mesh):
    n, nh = mesh.shape["frame"], mesh.shape["head"]

    def body(visual, w_key, w_value, queries, out_grad):
        rows, depth = visual.shape
        cols = w_key.shape[1]
        text, query_cols = queries.shape
        local_heads = query_cols // HEAD_DIM
        split = max(1, n // local_heads)
        part, width = text // split, query_cols * split // n
        vmem = pl.BlockSpec(memory_space=pltpu.VMEM)
        hbm = pl.BlockSpec(memory_space=pl.ANY)
        dn, dh = depth // n, depth // nh
        tile = dh // TILES
        slots = max(FAR, 2 * NEAR, 1)
        pairs = pltpu.SemaphoreType.DMA((2, n))
        dma = pltpu.SemaphoreType.DMA
        outs = pl.pallas_call(
            functools.partial(kernel, n, nh),
            out_shape=(
                pltpu.VMEM((text, query_cols), F32),
                pltpu.VMEM((dn, cols), F32),
                pltpu.VMEM((dn, cols), F32),
                pltpu.VMEM((rows, dh), F32),
            ),
            in_specs=[hbm] * 5,
            out_specs=(vmem,) * 4,
            scratch_shapes=[
                pltpu.VMEM((rows, depth), BF16),
                pltpu.VMEM((text, query_cols), F32),
                pltpu.VMEM((text, query_cols), F32),
                pltpu.VMEM((depth, cols), BF16),
                pltpu.VMEM((depth, cols), BF16),
                pltpu.VMEM((n, dn, rows), F32),
                pltpu.VMEM((n, dn, rows), F32),
                pltpu.VMEM((dn, n * rows), BF16),
                pltpu.VMEM((n, part, width), F32),
                pltpu.VMEM((n, part, width), F32),
                pltpu.VMEM((2, cols // HEAD_DIM, rows, HEAD_DIM), F32),
                pltpu.VMEM((2, n, rows, HEAD_DIM), F32),
                pltpu.VMEM((2, 2, n // 2, rows, HEAD_DIM), F32),
                pltpu.VMEM((2, n // 2, rows, HEAD_DIM), F32),
                pltpu.VMEM((2, n // 2, rows, HEAD_DIM), F32),
                pltpu.VMEM((2, rows, cols), F32),
                pltpu.VMEM((n, 2, rows, cols), F32),
                pltpu.VMEM((2, n * rows, cols), BF16),
                pltpu.VMEM((n, part, width), F32),
                pltpu.VMEM((n, part, width), F32),
                pltpu.VMEM((nh, TILES, rows, tile), F32),
                pltpu.VMEM((2, nh, TILES, rows, tile), F32),
                pltpu.VMEM((max(FAR + NEAR * (nh - 2), 1), 2, 2, tile // n, cols), F32),
                pltpu.VMEM((n, slots, 2, tile // n, cols), F32),
                pltpu.VMEM((2, 2, rows, cols), F32),
                dma((3,)),
                dma((2, CHUNKS)),
                pairs, pairs,
                dma((2, 2, n)),
                dma((len(UNITS), 2, n)),
                dma((2, 2, nh)),
                dma((2, 2)),
                dma((2, 2, n // 2)),
                pairs, pairs,
                dma((4, n)),
                dma((2, 2, nh, TILES)),
                dma((max(FAR + NEAR * (nh - 2), 1), 2)),
                dma((2, slots)),
                pairs,
                dma((2, 2)),
            ],
            compiler_params=pltpu.CompilerParams(
                collective_id=0, has_side_effects=True, vmem_limit_bytes=60000000
            ),
        )(visual, w_key, w_value, queries, out_grad)
        return pl.pallas_call(
            store,
            out_shape=tuple(jax.ShapeDtypeStruct(o.shape, o.dtype) for o in outs),
            in_specs=[vmem] * 4,
            out_specs=(hbm,) * 4,
            scratch_shapes=[dma((4,))],
            compiler_params=pltpu.CompilerParams(vmem_limit_bytes=1 << 20),
        )(*[pltpu.with_memory_space_constraint(o, pltpu.VMEM) for o in outs])

    return jax.shard_map(
        body,
        mesh=mesh,
        in_specs=(
            P("frame", None),
            P(None, "head"),
            P(None, "head"),
            P("frame", "head"),
            P("frame", "head"),
        ),
        out_specs=(P("frame", "head"), P("frame", "head"), P("frame", "head"), P("frame", "head")),
        check_vma=False,
    )
```

```python
import functools

import jax
import jax.numpy as jnp
from jax import lax
from jax.experimental import pallas as pl
from jax.experimental.pallas import tpu as pltpu
from jax.sharding import PartitionSpec as P

HEAD_DIM = 128
MESH = pl.DeviceIdType.MESH
CHUNKS = 8
TILES = 8
UNITS = (1, 1, 2, 2, 2)
FAR, NEAR = 4, 2
LAG, STORES = 3, 4
F32, BF16 = jnp.float32, jnp.bfloat16
LANES = (((1,), (1,)), ((), ()))


def halves(a):
    high = a.astype(BF16)
    return high, (a - high.astype(F32)).astype(BF16)


def product(a, b, dims):
    (ah, al), (bh, bl) = a, b
    dot = functools.partial(
        lax.dot_general, dimension_numbers=(dims, ((), ())), preferred_element_type=F32
    )
    return dot(ah, bh) + (dot(ah, bl) + dot(al, bh))


def kernel(
    n, nh, vis_any, wk_any, wv_any, q_any, g_any, qg_out, kwg_out, vwg_out, vg_out,
    vis, q, g, wk, wv, visf, visl, vist, ql, gl, kvs, kvl, parts, pre, partl, kgs, agl, kgb,
    qgs, qgl, vgp, zz, wst, wx, kgz, dsc,
    in_sems, w_sem, q_sems, g_sems, kv_sems, v_sems, vz_sems, pre_sems, part_sems, qg_sems, ag_sems,
    on_sems, z_sems, ws_sems, wz_sems, wx_sems, kz_sems, blk_sems,
):
    me, my_head = lax.axis_index("frame"), lax.axis_index("head")
    rows, depth = vis.shape
    cols = wk.shape[1]
    kv_local = cols // HEAD_DIM
    text_part, width = ql.shape[1], ql.shape[2]
    split = q.shape[0] // text_part
    heads = width // HEAD_DIM
    share = n // kv_local
    dn, dh = depth // n, depth // nh
    chunk = depth // CHUNKS
    tile = dh // TILES
    factor = HEAD_DIM ** (-0.5)
    bounds = [0]
    for u in UNITS:
        bounds.append(bounds[-1] + u * dn // sum(UNITS))
    ahead = [0] + [NEAR] * (nh - 2) + [FAR]

    def frame_copy_of(src, dst, send_sem, recv_sem, target):
        return pltpu.make_async_remote_copy(
            src_ref=src, dst_ref=dst, send_sem=send_sem, recv_sem=recv_sem,
            device_id={"frame": target}, device_id_type=MESH,
        )

    def frame_copy(src, dst, sems, slot_send, slot_recv, target):
        return frame_copy_of(src, dst, sems.at[0, slot_send], sems.at[1, slot_recv], target)

    def head_copy(src, dst, send_sem, recv_sem, target):
        return pltpu.make_async_remote_copy(
            src_ref=src, dst_ref=dst, send_sem=send_sem, recv_sem=recv_sem,
            device_id={"head": target}, device_id_type=MESH,
        )

    def peer(k):
        return lax.rem(me + k, n)

    def source(k):
        return lax.rem(me + n - k, n)

    core, chip, chips = lax.rem(me, 2), me // 2, n // 2
    sibling = me + 1 - 2 * core

    def mate(j):
        return lax.rem(me + 2 * j, n)

    def mate_source(j):
        return lax.rem(me + n - 2 * j, n)

    sends, late = [], []

    def send(copy, kept=sends):
        copy.start()
        kept.append(copy)

    def spread(pick, land, sems):
        send(frame_copy(pick(sibling), land.at[me], sems, sibling, me, sibling))
        for j in range(1, chips):
            p = mate(j)
            send(frame_copy(pick(p), land.at[me], sems, p, me, p))

    def forward(land, sems, on):
        for j in range(1, chips):
            s = mate_source(j)
            frame_copy(land.at[s], land.at[s], sems, s, s, s).wait_recv()
            send(frame_copy_of(land.at[s], land.at[s], on.at[s], sems.at[1, s], sibling))

    def wait_rest(land, sems):
        frame_copy(land.at[sibling], land.at[sibling], sems, sibling, sibling, sibling).wait_recv()
        for j in range(1, chips):
            s = lax.rem(sibling + n - 2 * j, n)
            frame_copy(land.at[s], land.at[s], sems, s, s, sibling).wait_recv()

    def wait_all(land, sems):
        for k in range(1, n):
            s = source(k)
            frame_copy(land.at[s], land.at[s], sems, s, s, s).wait_recv()

    def to_vmem(src, dst, sem):
        copy = pltpu.make_async_copy(src, dst, sem)
        copy.start()
        return copy

    texts_in = [to_vmem(q_any, q, in_sems.at[0]), to_vmem(g_any, g, in_sems.at[1])]
    vis_in = to_vmem(vis_any, vis, in_sems.at[2])
    loads = [
        [
            to_vmem(src.at[pl.ds(c * chunk, chunk)], dst.at[pl.ds(c * chunk, chunk)], w_sem.at[i, c])
            for c in range(CHUNKS)
        ]
        for i, (src, dst) in enumerate(((wk_any, wk), (wv_any, wv)))
    ]

    barrier = pltpu.get_barrier_semaphore()
    for k in range(1, n):
        pl.semaphore_signal(barrier, inc=1, device_id={"frame": peer(k)}, device_id_type=MESH)
    for j in range(1, nh):
        pl.semaphore_signal(
            barrier, inc=1, device_id={"head": lax.rem(my_head + j, nh)}, device_id_type=MESH
        )
    pl.semaphore_wait(barrier, n + nh - 2)

    def text_at(p):
        part, block = lax.rem(p, split), p // split
        return (
            pl.ds(pl.multiple_of(part * text_part, text_part), text_part),
            pl.ds(pl.multiple_of(block * width, width), width),
        )

    def send_text(copy, src, dst, sems):
        copy.wait()
        for k in range(1, n):
            p = peer(k)
            send(frame_copy(src.at[text_at(p)], dst.at[me], sems, p, me, p))
        dst[me] = src[text_at(me)]

    def project(i, w):
        acc = jnp.zeros((rows, cols), F32)
        for c in range(CHUNKS):
            if i == 0:
                loads[i][c].wait()
            at = pl.ds(c * chunk, chunk)
            acc += jnp.dot(vis[:, at], w[at], preferred_element_type=F32)
        for a in range(kv_local):
            kvs[i, a] = acc[:, a * HEAD_DIM : (a + 1) * HEAD_DIM]
        spread(lambda p: kvs.at[i, p // share], kvl.at[i], kv_sems.at[i])
        kvl[i, me] = kvs[i, me // share]

    quarter = bounds[1] // nh

    def quarter_at(h):
        return pl.ds(pl.multiple_of(h * quarter, quarter), quarter)

    def onward_head(way):
        return jnp.clip(my_head + 1 - 2 * way, 0, nh - 1)

    def can_go(way):
        return my_head < nh - 1 if way == 0 else my_head > 0

    def quarter_copy(way, s):
        land = visl.at[:, quarter_at(s)]
        return head_copy(land, land, vz_sems.at[0, way, s], vz_sems.at[1, way, s], onward_head(way))

    def turn_visual(i):
        at = slice(bounds[i], bounds[i + 1])
        for p in range(n):
            block = vis[:, p * dn + bounds[i] : p * dn + bounds[i + 1]]
            visf[p, at] = block.astype(F32).T
        if i > 0:
            visl[me, at] = visf[me, at]

    def share_visual():
        at = quarter_at(my_head)
        visl[me, at] = visf[me, at]
        for k in range(1, n):
            p = peer(k)
            send(frame_copy(visf.at[p, at], visl.at[me, at], v_sems.at[0], p, me, p))

    def pass_visual():
        at = quarter_at(my_head)
        for k in range(1, n):
            s = source(k)
            frame_copy(visl.at[s, at], visl.at[s, at], v_sems.at[0], s, s, s).wait_recv()
        for way in range(2):

            @pl.when(can_go(way))
            def _():
                quarter_copy(way, my_head).start()

    def relay_visual(j):
        for way in range(2):
            s = my_head - j if way == 0 else my_head + j

            @pl.when(jnp.logical_and(s >= 0, s < nh))
            def _():
                quarter_copy(way, jnp.clip(s, 0, nh - 1)).wait_recv()

                @pl.when(can_go(way))
                def _():
                    quarter_copy(way, jnp.clip(s, 0, nh - 1)).start()

    def send_visual(i):
        at = pl.ds(bounds[i], bounds[i + 1] - bounds[i])
        kept = late if i == len(UNITS) - 1 else sends
        for k in range(1, n):
            p = peer(k)
            send(frame_copy(visf.at[p, at], visl.at[me, at], v_sems.at[i], p, me, p), kept)

    def take_visual(i):
        at = pl.ds(bounds[i], bounds[i + 1] - bounds[i])
        if i > 0:
            for k in range(1, n):
                s = source(k)
                land = visl.at[s, at]
                frame_copy(land, land, v_sems.at[i], s, s, s).wait_recv()
        for s in range(n):
            vist[at, s * rows : (s + 1) * rows] = visl[s, at].astype(BF16)
        for j, out in enumerate((kwg_out, vwg_out)):
            out[at] = jnp.dot(vist[at], kgb[j], preferred_element_type=F32)

    is_end = jnp.logical_or(my_head == 0, my_head == nh - 1)
    staged = [(t, c) for t in range(nh - 1, 0, -1) for c in range(ahead[t])]
    slots = wx.shape[1]
    tw = tile // n

    def slot_of(t, c):
        return c if t == nh - 1 else jnp.where(my_head == 0, c, NEAR + c)

    square = chips == 4
    far_core = 6 - 2 * chip + core
    direct = (me, far_core) if square else (me,)

    def stage_copy(k, b):
        t, c = staged[k]
        d = jnp.where(my_head == 0, t, nh - 1 - t)
        return head_copy(
            wst.at[k, b], wx.at[direct[b], slot_of(t, c)], ws_sems.at[k, b],
            wz_sems.at[b, slot_of(t, c)], d,
        )

    send_text(texts_in[0], q, ql, q_sems)
    vis_in.wait()
    turn_visual(0)
    project(0, wk)
    for c in range(CHUNKS):
        loads[1][c].wait()
    if staged:

        @pl.when(is_end)
        def _():
            for k, (t, c) in enumerate(staged):
                d = jnp.where(my_head == 0, t, nh - 1 - t)
                for b, owner in enumerate(direct):
                    at = pl.ds(pl.multiple_of(d * dh + c * tile + owner * tw, tw), tw)
                    for i, w in enumerate((wk, wv)):
                        wst[k, b, i] = w[at].astype(F32)
                    stage_copy(k, b).start()

    send_text(texts_in[1], g, gl, g_sems)
    project(1, wv)
    share_visual()

    turn_visual(1)
    send_visual(1)
    for i in range(2, len(UNITS)):
        turn_visual(i)

    forward(kvl.at[0], kv_sems.at[0], on_sems.at[0])
    wait_all(ql, q_sems)
    wait_rest(kvl.at[0], kv_sems.at[0])
    keys = kvl[0].reshape(n * rows, HEAD_DIM)
    texts = [slice(h * HEAD_DIM, (h + 1) * HEAD_DIM) for h in range(heads)]
    queries = [ql[:, :, at].reshape(n * text_part, HEAD_DIM) for at in texts]
    probs = []
    for query in queries:
        scores = lax.dot_general(
            keys, query, LANES, precision=lax.Precision.HIGHEST, preferred_element_type=F32
        ) * factor
        raw = jnp.exp(scores - jnp.max(scores, axis=0, keepdims=True))
        probs.append(raw * (1.0 / jnp.sum(raw, axis=0, keepdims=True)))

    forward(kvl.at[1], kv_sems.at[1], on_sems.at[1])
    wait_all(gl, g_sems)
    grads2 = [halves(gl[:, :, at].reshape(n * text_part, HEAD_DIM)) for at in texts]

    def gather_ahead():
        for b, owner in enumerate(direct):
            for j in range(slots):
                land = wx.at[owner, j]
                head_copy(land, land, wz_sems.at[b, j], wz_sems.at[b, j], my_head).wait_recv()
        if square:
            for p in near_mates(me) + [sibling]:
                send(frame_copy(wx.at[me], wx.at[me], wx_sems, p, me, p))
            send(frame_copy_of(wx.at[far_core], wx.at[far_core], on_sems.at[3, far_core], wx_sems.at[1, far_core], sibling))
        else:
            spread(lambda p: wx.at[me], wx, wx_sems)

    def near_mates(d):
        c, b = d // 2, lax.rem(d, 2)
        return [2 * (c + 1 - 2 * lax.rem(c, 2)) + b, 2 * lax.rem(c + 2, 4) + b]

    def forward_ahead():
        if not square:
            forward(wx, wx_sems, on_sems.at[3])
            wait_rest(wx, wx_sems)
            return
        for s in near_mates(me):
            frame_copy(wx.at[s], wx.at[s], wx_sems, s, s, s).wait_recv()
            send(frame_copy_of(wx.at[s], wx.at[s], on_sems.at[3, s], wx_sems.at[1, s], sibling))

    def rest_ahead():
        if square:
            for s in near_mates(sibling) + [sibling, far_core + 1 - 2 * core]:
                frame_copy(wx.at[s], wx.at[s], wx_sems, s, s, sibling).wait_recv()

    def total(terms):
        out = terms[0]
        for term in terms[1:]:
            out = out + term
        return out

    def exchange(i):
        return frame_copy_of(
            parts.at[i, 1 - core], pre.at[i], pre_sems.at[i, 0], pre_sems.at[i, 1], sibling
        )

    def give(i, part):
        part = part.reshape(chips, 2, rows, HEAD_DIM)
        for c in range(2):
            parts[i, c] = part[:, c]
        send(exchange(i))

    def pass_on(i):
        exchange(i).wait_recv()
        parts[i, core] += pre[i]
        for j in range(1, chips):
            p = mate(j)
            send(
                frame_copy(
                    parts.at[i, core, p // 2], partl.at[i, chip], part_sems.at[i], p // 2, chip, p
                )
            )
        partl[i, chip] = parts[i, core, chip]

    give(1, total([product(halves(p), g2, ((1,), (0,))) for p, g2 in zip(probs, grads2)]))

    wait_rest(kvl.at[1], kv_sems.at[1])
    values2 = halves(kvl[1].reshape(n * rows, HEAD_DIM))
    dscores2 = []
    for h, (p, g2) in enumerate(zip(probs, grads2)):
        dprob = product(values2, g2, ((1,), (1,)))
        delta = jnp.sum(p * dprob, axis=0, keepdims=True)
        dscores2.append(halves(p * (dprob - delta)))
        if h == 0:
            pass_on(1)
    for h, d2 in enumerate(dscores2):
        for i in range(2):
            dsc[h, i] = d2[i]
    queries2 = [halves(query) for query in queries]

    def exchange_block(c):
        return frame_copy_of(
            parts.at[0, 1 - core, c], pre.at[0, c], blk_sems.at[0, c], blk_sems.at[1, c], sibling
        )

    def key_block(c):
        at = pl.ds(pl.multiple_of(c * 2 * rows, 2 * rows), 2 * rows)
        part = total(
            [
                product((dsc[h, 0, at], dsc[h, 1, at]), q2, ((1,), (0,)))
                for h, q2 in enumerate(queries2)
            ]
        )
        for k in range(2):
            parts[0, k, c] = part[k * rows : (k + 1) * rows]
        send(exchange_block(c))

    def pass_block(c, p):
        exchange_block(c).wait_recv()
        parts[0, core, c] += pre[0, c]
        if p is None:
            partl[0, chip] = parts[0, core, c]
        else:
            send(frame_copy(parts.at[0, core, c], partl.at[0, chip], part_sems.at[0], c, chip, p))

    blocks = [(mate(j) // 2, mate(j)) for j in range(1, chips)] + [(chip, None)]
    for k, (c, p) in enumerate(blocks):
        key_block(c)
        if k > 0:
            pass_block(*blocks[k - 1])
    pass_block(*blocks[-1])
    pass_visual()
    keys_t = halves(keys.T)
    for d2, at in zip(dscores2, texts):
        query_term = product(keys_t, d2, ((1,), (0,))).T * factor
        qgs[:, :, at] = query_term.reshape(n, text_part, HEAD_DIM)
    send_visual(2)

    low = [None, None]
    for i in (1, 0):
        for j in range(1, chips):
            s = mate_source(j)
            land = partl.at[i, s // 2]
            frame_copy(land, land, part_sems.at[i], s // 2, s // 2, s).wait_recv()
        for a in range(kv_local):
            column = total([partl[i, p] for p in range(a * share // 2, (a + 1) * share // 2)])
            if i == 0:
                column = column * factor
            kgs[i, :, a * HEAD_DIM : (a + 1) * HEAD_DIM] = column.astype(BF16).astype(F32)
        low[i] = kgs[i].astype(BF16)

    lead = jnp.where(2 * my_head < nh, 0, 1)

    def block_of(way, t):
        return jnp.where(way == 0, t, nh - 1 - t)

    def rank(way):
        return jnp.where(way == 0, my_head, nh - 1 - my_head)

    def visual_term(d, c):
        at = pl.ds(pl.multiple_of(d * dh + c * tile, tile), tile)
        vgp[d, c] = lax.dot_general(
            low[0], wk[at], LANES, preferred_element_type=F32
        ) + lax.dot_general(low[1], wv[at], LANES, preferred_element_type=F32)

    def hop(way, d, c):
        return head_copy(
            vgp.at[d, c], zz.at[way, d, c], z_sems.at[way, 0, d, c], z_sems.at[way, 1, d, c],
            onward_head(way),
        )

    def starts(t, c):
        return 1 if c < ahead[t] else 0

    def relay(way, t, c):
        d, first = block_of(way, t), starts(t, c)

        @pl.when(jnp.logical_and(rank(way) < t, rank(way) >= first))
        def _():
            @pl.when(rank(way) > first)
            def _():
                hop(way, d, c).wait_recv()
                vgp[d, c] += zz[way, d, c]

            hop(way, d, c).start()

    def kg_hop(way, first):
        return head_copy(
            kgs if first else kgz.at[way], kgz.at[way], kz_sems.at[way, 0], kz_sems.at[way, 1],
            onward_head(way),
        )

    def start_grads(way):
        @pl.when(rank(way) == 0)
        def _():
            kg_hop(way, True).start()

    def relay_grads(way):
        @pl.when(jnp.logical_and(rank(way) > 0, rank(way) < nh - 1))
        def _():
            kg_hop(way, False).wait_recv()
            kg_hop(way, False).start()

    def add_ahead():
        for way in range(2):

            @pl.when(rank(way) == nh - 1)
            def _():
                kg_hop(way, False).wait_recv()

        rest_ahead()
        for j in range(slots):
            from_right = jnp.where(is_end, jnp.where(my_head == 0, 1, 0), 1 if j >= NEAR else 0)
            c = jnp.where(is_end, j, j % NEAR)
            term = vgp[my_head, c]
            for i in range(2):
                block = wx[:, j, i].reshape(tile, cols).astype(BF16)
                term += lax.dot_general(
                    kgz[from_right, i].astype(BF16), block, LANES, preferred_element_type=F32
                )
            vgp[my_head, c] = term

    def send_rows():
        spread(lambda p: kgs, agl, ag_sems)
        agl[me] = kgs[...]
        for k in range(1, n):
            p = peer(k)
            send(frame_copy(qgs.at[p], qgl.at[me], qg_sems, p, me, p))
        qgl[me] = qgs[me]
        if staged:
            gather_ahead()
        for i in range(3, len(UNITS)):
            send_visual(i)

    order = [(t, c) for t in range(nh - 1, 0, -1) for c in range(TILES)]

    def visual_terms(way, t, c):
        @pl.when(rank(way) >= starts(t, c))
        def _():
            visual_term(block_of(way, t), c)

    if staged:
        start_grads(lead)
    for k in range(len(order) + LAG):
        if k < len(order):
            t, c = order[k]
            if 2 * t > nh - 1:
                visual_terms(lead, t, c)
                visual_terms(1 - lead, t, c)
            if k == FAR:
                if staged:
                    relay_grads(lead)
            relay(lead, t, c)
        if k >= LAG:
            if k - LAG == TILES and staged:
                relay_grads(1 - lead)
            relay(1 - lead, *order[k - LAG])
        if k == FAR - 1:
            send_rows()
        if k == FAR:
            relay_visual(1)
        if k == TILES + 2 and nh > 2:
            relay_visual(2)

    def wait_hops(some):
        for way in (lead, 1 - lead):
            for t, c in some:

                @pl.when(jnp.logical_and(rank(way) < t, rank(way) >= starts(t, c)))
                def _():
                    hop(way, block_of(way, t), c).wait_send()

    for j in range(3, nh):
        relay_visual(j)
    forward(agl, ag_sems, on_sems.at[2])
    if staged:
        forward_ahead()
    wait_rest(agl, ag_sems)
    for i in range(2):
        kgb[i] = agl[:, i].reshape(n * rows, cols).astype(BF16)
    for i in range(3):
        take_visual(i)
    wait_all(qgl, qg_sems)
    for s in range(n):
        part, block = s % split, s // split
        qg_out[
            part * text_part : (part + 1) * text_part, block * width : (block + 1) * width
        ] = qgl[s]
    if staged:
        add_ahead()
    for i in range(3, len(UNITS) - 1):
        take_visual(i)
    for copy in sends:
        copy.wait_send()
    wait_hops(order[: 2 * TILES])
    take_visual(len(UNITS) - 1)

    for c in range(TILES):
        at = slice(c * tile, (c + 1) * tile)
        vg_out[:, at] = vgp[my_head, c]
        for way in (lead, 1 - lead):
            t = rank(way)
            count = jnp.where(t == nh - 1, FAR, NEAR)

            @pl.when(t > jnp.where(c < count, 1, 0))
            def _():
                hop(way, my_head, c).wait_recv()
                vg_out[:, at] += zz[way, my_head, c]

    wait_hops(order[2 * TILES :])
    for way in (lead, 1 - lead):
        if staged:

            @pl.when(rank(way) < nh - 1)
            def _():
                kg_hop(way, True).wait_send()

    if staged:

        @pl.when(is_end)
        def _():
            for k in range(len(staged)):
                for b in range(len(direct)):
                    stage_copy(k, b).wait_send()

    for way in range(2):
        for j in range(nh):
            s = my_head - j if way == 0 else my_head + j

            @pl.when(jnp.logical_and(jnp.logical_and(s >= 0, s < nh), can_go(way)))
            def _():
                quarter_copy(way, jnp.clip(s, 0, nh - 1)).wait_send()

    for copy in late:
        copy.wait_send()


def store(*refs):
    outs, sems = refs[len(refs) // 2 : -1], refs[-1]
    copies = []
    for i, (src, dst) in enumerate(zip(refs, outs)):
        step = src.shape[0] // STORES
        for k in range(STORES):
            at = pl.ds(k * step, step)
            copies.append(pltpu.make_async_copy(src.at[at], dst.at[at], sems.at[i, k]))
    for copy in copies:
        copy.start()
    for copy in copies:
        copy.wait()


def solution(mesh):
    n, nh = mesh.shape["frame"], mesh.shape["head"]

    def body(visual, w_key, w_value, queries, out_grad):
        rows, depth = visual.shape
        cols = w_key.shape[1]
        text, query_cols = queries.shape
        local_heads = query_cols // HEAD_DIM
        split = max(1, n // local_heads)
        part, width = text // split, query_cols * split // n
        vmem = pl.BlockSpec(memory_space=pltpu.VMEM)
        hbm = pl.BlockSpec(memory_space=pl.ANY)
        dn, dh = depth // n, depth // nh
        tile = dh // TILES
        slots = max(FAR, 2 * NEAR, 1)
        pairs = pltpu.SemaphoreType.DMA((2, n))
        dma = pltpu.SemaphoreType.DMA
        outs = pl.pallas_call(
            functools.partial(kernel, n, nh),
            out_shape=(
                pltpu.VMEM((text, query_cols), F32),
                pltpu.VMEM((dn, cols), F32),
                pltpu.VMEM((dn, cols), F32),
                pltpu.VMEM((rows, dh), F32),
            ),
            in_specs=[hbm] * 5,
            out_specs=(vmem,) * 4,
            scratch_shapes=[
                pltpu.VMEM((rows, depth), BF16),
                pltpu.VMEM((text, query_cols), F32),
                pltpu.VMEM((text, query_cols), F32),
                pltpu.VMEM((depth, cols), BF16),
                pltpu.VMEM((depth, cols), BF16),
                pltpu.VMEM((n, dn, rows), F32),
                pltpu.VMEM((n, dn, rows), F32),
                pltpu.VMEM((dn, n * rows), BF16),
                pltpu.VMEM((n, part, width), F32),
                pltpu.VMEM((n, part, width), F32),
                pltpu.VMEM((2, cols // HEAD_DIM, rows, HEAD_DIM), F32),
                pltpu.VMEM((2, n, rows, HEAD_DIM), F32),
                pltpu.VMEM((2, 2, n // 2, rows, HEAD_DIM), F32),
                pltpu.VMEM((2, n // 2, rows, HEAD_DIM), F32),
                pltpu.VMEM((2, n // 2, rows, HEAD_DIM), F32),
                pltpu.VMEM((2, rows, cols), F32),
                pltpu.VMEM((n, 2, rows, cols), F32),
                pltpu.VMEM((2, n * rows, cols), BF16),
                pltpu.VMEM((n, part, width), F32),
                pltpu.VMEM((n, part, width), F32),
                pltpu.VMEM((nh, TILES, rows, tile), F32),
                pltpu.VMEM((2, nh, TILES, rows, tile), F32),
                pltpu.VMEM((max(FAR + NEAR * (nh - 2), 1), 2, 2, tile // n, cols), F32),
                pltpu.VMEM((n, slots, 2, tile // n, cols), F32),
                pltpu.VMEM((2, 2, rows, cols), F32),
                pltpu.VMEM((width // HEAD_DIM, 2, n * rows, part * n), BF16),
                dma((3,)),
                dma((2, CHUNKS)),
                pairs, pairs,
                dma((2, 2, n)),
                dma((len(UNITS), 2, n)),
                dma((2, 2, nh)),
                dma((2, 2)),
                dma((2, 2, n // 2)),
                pairs, pairs,
                dma((4, n)),
                dma((2, 2, nh, TILES)),
                dma((max(FAR + NEAR * (nh - 2), 1), 2)),
                dma((2, slots)),
                pairs,
                dma((2, 2)),
                dma((2, n // 2)),
            ],
            compiler_params=pltpu.CompilerParams(
                collective_id=0, has_side_effects=True, vmem_limit_bytes=60000000
            ),
        )(visual, w_key, w_value, queries, out_grad)
        return pl.pallas_call(
            store,
            out_shape=tuple(jax.ShapeDtypeStruct(o.shape, o.dtype) for o in outs),
            in_specs=[vmem] * 4,
            out_specs=(hbm,) * 4,
            scratch_shapes=[dma((4, STORES))],
            compiler_params=pltpu.CompilerParams(vmem_limit_bytes=1 << 20),
        )(*[pltpu.with_memory_space_constraint(o, pltpu.VMEM) for o in outs])

    return jax.shard_map(
        body,
        mesh=mesh,
        in_specs=(
            P("frame", None),
            P(None, "head"),
            P(None, "head"),
            P("frame", "head"),
            P("frame", "head"),
        ),
        out_specs=(P("frame", "head"), P("frame", "head"), P("frame", "head"), P("frame", "head")),
        check_vma=False,
    )
```

```python
import functools

import jax
import jax.numpy as jnp
from jax import lax
from jax.experimental import pallas as pl
from jax.experimental.pallas import tpu as pltpu
from jax.sharding import PartitionSpec as P

HEAD_DIM = 128
MESH = pl.DeviceIdType.MESH
CHUNKS = 8
TILES = 8
UNITS = (1, 1, 2, 2, 2)
FAR, NEAR = 4, 2
LAG, STORES = 2, 4
F32, BF16 = jnp.float32, jnp.bfloat16
LANES = (((1,), (1,)), ((), ()))


def halves(a):
    high = a.astype(BF16)
    return high, (a - high.astype(F32)).astype(BF16)


def product(a, b, dims):
    (ah, al), (bh, bl) = a, b
    dot = functools.partial(
        lax.dot_general, dimension_numbers=(dims, ((), ())), preferred_element_type=F32
    )
    return dot(ah, bh) + (dot(ah, bl) + dot(al, bh))


def kernel(
    n, nh, vis_any, wk_any, wv_any, q_any, g_any, qg_out, kwg_out, vwg_out, vg_out,
    vis, q, g, wk, wv, visf, visl, vist, ql, gl, kvs, kvl, parts, pre, partl, kgs, agl, kgb,
    qgs, qgl, vgp, zz, wst, wx, kgz, dsc,
    in_sems, w_sem, q_sems, g_sems, kv_sems, v_sems, vz_sems, pre_sems, part_sems, qg_sems, ag_sems,
    on_sems, z_sems, ws_sems, wz_sems, wx_sems, kz_sems, blk_sems,
):
    me, my_head = lax.axis_index("frame"), lax.axis_index("head")
    rows, depth = vis.shape
    cols = wk.shape[1]
    kv_local = cols // HEAD_DIM
    text_part, width = ql.shape[1], ql.shape[2]
    split = q.shape[0] // text_part
    heads = width // HEAD_DIM
    share = n // kv_local
    dn, dh = depth // n, depth // nh
    chunk = depth // CHUNKS
    tile = dh // TILES
    factor = HEAD_DIM ** (-0.5)
    bounds = [0]
    for u in UNITS:
        bounds.append(bounds[-1] + u * dn // sum(UNITS))
    ahead = [0] + [NEAR] * (nh - 2) + [FAR]

    def frame_copy_of(src, dst, send_sem, recv_sem, target):
        return pltpu.make_async_remote_copy(
            src_ref=src, dst_ref=dst, send_sem=send_sem, recv_sem=recv_sem,
            device_id={"frame": target}, device_id_type=MESH,
        )

    def frame_copy(src, dst, sems, slot_send, slot_recv, target):
        return frame_copy_of(src, dst, sems.at[0, slot_send], sems.at[1, slot_recv], target)

    def head_copy(src, dst, send_sem, recv_sem, target):
        return pltpu.make_async_remote_copy(
            src_ref=src, dst_ref=dst, send_sem=send_sem, recv_sem=recv_sem,
            device_id={"head": target}, device_id_type=MESH,
        )

    def peer(k):
        return lax.rem(me + k, n)

    def source(k):
        return lax.rem(me + n - k, n)

    core, chip, chips = lax.rem(me, 2), me // 2, n // 2
    sibling = me + 1 - 2 * core

    def mate(j):
        return lax.rem(me + 2 * j, n)

    def mate_source(j):
        return lax.rem(me + n - 2 * j, n)

    sends, late = [], []

    def send(copy, kept=sends):
        copy.start()
        kept.append(copy)

    def spread(pick, land, sems):
        send(frame_copy(pick(sibling), land.at[me], sems, sibling, me, sibling))
        for j in range(1, chips):
            p = mate(j)
            send(frame_copy(pick(p), land.at[me], sems, p, me, p))

    def forward(land, sems, on):
        for j in range(1, chips):
            s = mate_source(j)
            frame_copy(land.at[s], land.at[s], sems, s, s, s).wait_recv()
            send(frame_copy_of(land.at[s], land.at[s], on.at[s], sems.at[1, s], sibling))

    def wait_rest(land, sems):
        frame_copy(land.at[sibling], land.at[sibling], sems, sibling, sibling, sibling).wait_recv()
        for j in range(1, chips):
            s = lax.rem(sibling + n - 2 * j, n)
            frame_copy(land.at[s], land.at[s], sems, s, s, sibling).wait_recv()

    def wait_all(land, sems):
        for k in range(1, n):
            s = source(k)
            frame_copy(land.at[s], land.at[s], sems, s, s, s).wait_recv()

    def to_vmem(src, dst, sem):
        copy = pltpu.make_async_copy(src, dst, sem)
        copy.start()
        return copy

    texts_in = [to_vmem(q_any, q, in_sems.at[0]), to_vmem(g_any, g, in_sems.at[1])]
    vis_in = to_vmem(vis_any, vis, in_sems.at[2])
    loads = [
        [
            to_vmem(src.at[pl.ds(c * chunk, chunk)], dst.at[pl.ds(c * chunk, chunk)], w_sem.at[i, c])
            for c in range(CHUNKS)
        ]
        for i, (src, dst) in enumerate(((wk_any, wk), (wv_any, wv)))
    ]

    barrier = pltpu.get_barrier_semaphore()
    for k in range(1, n):
        pl.semaphore_signal(barrier, inc=1, device_id={"frame": peer(k)}, device_id_type=MESH)
    for j in range(1, nh):
        pl.semaphore_signal(
            barrier, inc=1, device_id={"head": lax.rem(my_head + j, nh)}, device_id_type=MESH
        )
    pl.semaphore_wait(barrier, n + nh - 2)

    def text_at(p):
        part, block = lax.rem(p, split), p // split
        return (
            pl.ds(pl.multiple_of(part * text_part, text_part), text_part),
            pl.ds(pl.multiple_of(block * width, width), width),
        )

    def send_text(copy, src, dst, sems):
        copy.wait()
        for k in range(1, n):
            p = peer(k)
            send(frame_copy(src.at[text_at(p)], dst.at[me], sems, p, me, p))
        dst[me] = src[text_at(me)]

    def project(i, w):
        acc = jnp.zeros((rows, cols), F32)
        for c in range(CHUNKS):
            if i == 0:
                loads[i][c].wait()
            at = pl.ds(c * chunk, chunk)
            acc += jnp.dot(vis[:, at], w[at], preferred_element_type=F32)
        for a in range(kv_local):
            kvs[i, a] = acc[:, a * HEAD_DIM : (a + 1) * HEAD_DIM]
        spread(lambda p: kvs.at[i, p // share], kvl.at[i], kv_sems.at[i])
        kvl[i, me] = kvs[i, me // share]

    quarter = bounds[1] // nh

    def quarter_at(h):
        return pl.ds(pl.multiple_of(h * quarter, quarter), quarter)

    def onward_head(way):
        return jnp.clip(my_head + 1 - 2 * way, 0, nh - 1)

    def can_go(way):
        return my_head < nh - 1 if way == 0 else my_head > 0

    def quarter_copy(way, s):
        land = visl.at[:, quarter_at(s)]
        return head_copy(land, land, vz_sems.at[0, way, s], vz_sems.at[1, way, s], onward_head(way))

    def turn_visual(i):
        at = slice(bounds[i], bounds[i + 1])
        for p in range(n):
            block = vis[:, p * dn + bounds[i] : p * dn + bounds[i + 1]]
            visf[p, at] = block.astype(F32).T
        if i > 0:
            visl[me, at] = visf[me, at]

    def share_visual():
        at = quarter_at(my_head)
        visl[me, at] = visf[me, at]
        for k in range(1, n):
            p = peer(k)
            send(frame_copy(visf.at[p, at], visl.at[me, at], v_sems.at[0], p, me, p))

    def pass_visual():
        at = quarter_at(my_head)
        for k in range(1, n):
            s = source(k)
            frame_copy(visl.at[s, at], visl.at[s, at], v_sems.at[0], s, s, s).wait_recv()
        for way in range(2):

            @pl.when(can_go(way))
            def _():
                quarter_copy(way, my_head).start()

    def relay_visual(j):
        for way in range(2):
            s = my_head - j if way == 0 else my_head + j

            @pl.when(jnp.logical_and(s >= 0, s < nh))
            def _():
                quarter_copy(way, jnp.clip(s, 0, nh - 1)).wait_recv()

                @pl.when(can_go(way))
                def _():
                    quarter_copy(way, jnp.clip(s, 0, nh - 1)).start()

    def send_visual(i):
        at = pl.ds(bounds[i], bounds[i + 1] - bounds[i])
        kept = late if i == len(UNITS) - 1 else sends
        for k in range(1, n):
            p = peer(k)
            send(frame_copy(visf.at[p, at], visl.at[me, at], v_sems.at[i], p, me, p), kept)

    def take_visual(i):
        at = pl.ds(bounds[i], bounds[i + 1] - bounds[i])
        if i > 0:
            for k in range(1, n):
                s = source(k)
                land = visl.at[s, at]
                frame_copy(land, land, v_sems.at[i], s, s, s).wait_recv()
        for s in range(n):
            vist[at, s * rows : (s + 1) * rows] = visl[s, at].astype(BF16)
        for j, out in enumerate((kwg_out, vwg_out)):
            out[at] = jnp.dot(vist[at], kgb[j], preferred_element_type=F32)

    is_end = jnp.logical_or(my_head == 0, my_head == nh - 1)
    staged = [(t, c) for t in range(nh - 1, 0, -1) for c in range(ahead[t])]
    slots = wx.shape[1]
    tw = tile // n

    def slot_of(t, c):
        return c if t == nh - 1 else jnp.where(my_head == 0, c, NEAR + c)

    square = chips == 4
    far_core = 6 - 2 * chip + core
    direct = (me, far_core) if square else (me,)

    def stage_copy(k, b):
        t, c = staged[k]
        d = jnp.where(my_head == 0, t, nh - 1 - t)
        return head_copy(
            wst.at[k, b], wx.at[direct[b], slot_of(t, c)], ws_sems.at[k, b],
            wz_sems.at[b, slot_of(t, c)], d,
        )

    send_text(texts_in[0], q, ql, q_sems)
    vis_in.wait()
    project(0, wk)
    send_text(texts_in[1], g, gl, g_sems)
    for c in range(CHUNKS):
        loads[1][c].wait()
    if staged:

        @pl.when(is_end)
        def _():
            for k, (t, c) in enumerate(staged):
                d = jnp.where(my_head == 0, t, nh - 1 - t)
                for b, owner in enumerate(direct):
                    at = pl.ds(pl.multiple_of(d * dh + c * tile + owner * tw, tw), tw)
                    for i, w in enumerate((wk, wv)):
                        wst[k, b, i] = w[at].astype(F32)
                    stage_copy(k, b).start()

    project(1, wv)
    turn_visual(0)
    share_visual()

    turn_visual(1)
    send_visual(1)
    for i in range(2, len(UNITS)):
        turn_visual(i)

    forward(kvl.at[0], kv_sems.at[0], on_sems.at[0])
    wait_all(ql, q_sems)
    wait_rest(kvl.at[0], kv_sems.at[0])
    keys = kvl[0].reshape(n * rows, HEAD_DIM)
    texts = [slice(h * HEAD_DIM, (h + 1) * HEAD_DIM) for h in range(heads)]
    queries = [ql[:, :, at].reshape(n * text_part, HEAD_DIM) for at in texts]
    probs = []
    for query in queries:
        scores = lax.dot_general(
            keys, query, LANES, precision=lax.Precision.HIGHEST, preferred_element_type=F32
        ) * factor
        raw = jnp.exp(scores - jnp.max(scores, axis=0, keepdims=True))
        probs.append(raw * (1.0 / jnp.sum(raw, axis=0, keepdims=True)))

    forward(kvl.at[1], kv_sems.at[1], on_sems.at[1])
    wait_all(gl, g_sems)
    grads2 = [halves(gl[:, :, at].reshape(n * text_part, HEAD_DIM)) for at in texts]

    def gather_ahead():
        for b, owner in enumerate(direct):
            for j in range(slots):
                land = wx.at[owner, j]
                head_copy(land, land, wz_sems.at[b, j], wz_sems.at[b, j], my_head).wait_recv()
        if square:
            for p in near_mates(me) + [sibling]:
                send(frame_copy(wx.at[me], wx.at[me], wx_sems, p, me, p))
            send(frame_copy_of(wx.at[far_core], wx.at[far_core], on_sems.at[3, far_core], wx_sems.at[1, far_core], sibling))
        else:
            spread(lambda p: wx.at[me], wx, wx_sems)

    def near_mates(d):
        c, b = d // 2, lax.rem(d, 2)
        return [2 * (c + 1 - 2 * lax.rem(c, 2)) + b, 2 * lax.rem(c + 2, 4) + b]

    def forward_ahead():
        if not square:
            forward(wx, wx_sems, on_sems.at[3])
            wait_rest(wx, wx_sems)
            return
        for s in near_mates(me):
            frame_copy(wx.at[s], wx.at[s], wx_sems, s, s, s).wait_recv()
            send(frame_copy_of(wx.at[s], wx.at[s], on_sems.at[3, s], wx_sems.at[1, s], sibling))

    def rest_ahead():
        if square:
            for s in near_mates(sibling) + [sibling, far_core + 1 - 2 * core]:
                frame_copy(wx.at[s], wx.at[s], wx_sems, s, s, sibling).wait_recv()

    def total(terms):
        out = terms[0]
        for term in terms[1:]:
            out = out + term
        return out

    def exchange(i):
        return frame_copy_of(
            parts.at[i, 1 - core], pre.at[i], pre_sems.at[i, 0], pre_sems.at[i, 1], sibling
        )

    def give(i, part):
        part = part.reshape(chips, 2, rows, HEAD_DIM)
        for c in range(2):
            parts[i, c] = part[:, c]
        send(exchange(i))

    def pass_on(i):
        exchange(i).wait_recv()
        parts[i, core] += pre[i]
        for j in range(1, chips):
            p = mate(j)
            send(
                frame_copy(
                    parts.at[i, core, p // 2], partl.at[i, chip], part_sems.at[i], p // 2, chip, p
                )
            )
        partl[i, chip] = parts[i, core, chip]

    give(1, total([product(halves(p), g2, ((1,), (0,))) for p, g2 in zip(probs, grads2)]))

    wait_rest(kvl.at[1], kv_sems.at[1])
    values2 = halves(kvl[1].reshape(n * rows, HEAD_DIM))
    dscores2 = []
    for h, (p, g2) in enumerate(zip(probs, grads2)):
        dprob = product(values2, g2, ((1,), (1,)))
        delta = jnp.sum(p * dprob, axis=0, keepdims=True)
        dscores2.append(halves(p * (dprob - delta)))
        if h == 0:
            pass_on(1)
    for h, d2 in enumerate(dscores2):
        for i in range(2):
            dsc[h, i] = d2[i]
    queries2 = [halves(query) for query in queries]

    def exchange_block(c):
        return frame_copy_of(
            parts.at[0, 1 - core, c], pre.at[0, c], blk_sems.at[0, c], blk_sems.at[1, c], sibling
        )

    def key_block(c):
        at = pl.ds(pl.multiple_of(c * 2 * rows, 2 * rows), 2 * rows)
        part = total(
            [
                product((dsc[h, 0, at], dsc[h, 1, at]), q2, ((1,), (0,)))
                for h, q2 in enumerate(queries2)
            ]
        )
        for k in range(2):
            parts[0, k, c] = part[k * rows : (k + 1) * rows]
        send(exchange_block(c))

    def pass_block(c, p):
        exchange_block(c).wait_recv()
        parts[0, core, c] += pre[0, c]
        if p is None:
            partl[0, chip] = parts[0, core, c]
        else:
            send(frame_copy(parts.at[0, core, c], partl.at[0, chip], part_sems.at[0], c, chip, p))

    blocks = [(mate(j) // 2, mate(j)) for j in range(1, chips)] + [(chip, None)]
    for k, (c, p) in enumerate(blocks):
        key_block(c)
        if k > 0:
            pass_block(*blocks[k - 1])
    pass_block(*blocks[-1])
    pass_visual()
    keys_t = halves(keys.T)
    for d2, at in zip(dscores2, texts):
        query_term = product(keys_t, d2, ((1,), (0,))).T * factor
        qgs[:, :, at] = query_term.reshape(n, text_part, HEAD_DIM)
    send_visual(2)

    low = [None, None]
    for i in (1, 0):
        for j in range(1, chips):
            s = mate_source(j)
            land = partl.at[i, s // 2]
            frame_copy(land, land, part_sems.at[i], s // 2, s // 2, s).wait_recv()
        for a in range(kv_local):
            column = total([partl[i, p] for p in range(a * share // 2, (a + 1) * share // 2)])
            if i == 0:
                column = column * factor
            kgs[i, :, a * HEAD_DIM : (a + 1) * HEAD_DIM] = column.astype(BF16).astype(F32)
        low[i] = kgs[i].astype(BF16)

    lead = jnp.where(2 * my_head < nh, 0, 1)

    def block_of(way, t):
        return jnp.where(way == 0, t, nh - 1 - t)

    def rank(way):
        return jnp.where(way == 0, my_head, nh - 1 - my_head)

    def visual_term(d, c):
        at = pl.ds(pl.multiple_of(d * dh + c * tile, tile), tile)
        vgp[d, c] = lax.dot_general(
            low[0], wk[at], LANES, preferred_element_type=F32
        ) + lax.dot_general(low[1], wv[at], LANES, preferred_element_type=F32)

    def hop(way, d, c):
        return head_copy(
            vgp.at[d, c], zz.at[way, d, c], z_sems.at[way, 0, d, c], z_sems.at[way, 1, d, c],
            onward_head(way),
        )

    def starts(t, c):
        return 1 if c < ahead[t] else 0

    def relay(way, t, c):
        d, first = block_of(way, t), starts(t, c)

        @pl.when(jnp.logical_and(rank(way) < t, rank(way) >= first))
        def _():
            @pl.when(rank(way) > first)
            def _():
                hop(way, d, c).wait_recv()
                vgp[d, c] += zz[way, d, c]

            hop(way, d, c).start()

    def kg_hop(way, first):
        return head_copy(
            kgs if first else kgz.at[way], kgz.at[way], kz_sems.at[way, 0], kz_sems.at[way, 1],
            onward_head(way),
        )

    def start_grads(way):
        @pl.when(rank(way) == 0)
        def _():
            kg_hop(way, True).start()

    def relay_grads(way):
        @pl.when(jnp.logical_and(rank(way) > 0, rank(way) < nh - 1))
        def _():
            kg_hop(way, False).wait_recv()
            kg_hop(way, False).start()

    def add_ahead():
        for way in range(2):

            @pl.when(rank(way) == nh - 1)
            def _():
                kg_hop(way, False).wait_recv()

        rest_ahead()
        for j in range(slots):
            from_right = jnp.where(is_end, jnp.where(my_head == 0, 1, 0), 1 if j >= NEAR else 0)
            c = jnp.where(is_end, j, j % NEAR)
            term = vgp[my_head, c]
            for i in range(2):
                block = wx[:, j, i].reshape(tile, cols).astype(BF16)
                term += lax.dot_general(
                    kgz[from_right, i].astype(BF16), block, LANES, preferred_element_type=F32
                )
            vgp[my_head, c] = term

    def send_rows():
        spread(lambda p: kgs, agl, ag_sems)
        agl[me] = kgs[...]
        for k in range(1, n):
            p = peer(k)
            send(frame_copy(qgs.at[p], qgl.at[me], qg_sems, p, me, p))
        qgl[me] = qgs[me]
        if staged:
            gather_ahead()
        for i in range(3, len(UNITS)):
            send_visual(i)

    order = [(t, c) for t in range(nh - 1, 0, -1) for c in range(TILES)]

    def visual_terms(way, t, c):
        @pl.when(rank(way) >= starts(t, c))
        def _():
            visual_term(block_of(way, t), c)

    if staged:
        start_grads(lead)
    for k in range(len(order) + LAG):
        if k < len(order):
            t, c = order[k]
            if 2 * t > nh - 1:
                visual_terms(lead, t, c)
                visual_terms(1 - lead, t, c)
            if k == FAR:
                if staged:
                    relay_grads(lead)
            relay(lead, t, c)
        if k >= LAG:
            if k - LAG == TILES and staged:
                relay_grads(1 - lead)
            relay(1 - lead, *order[k - LAG])
        if k == FAR - 1:
            send_rows()
        if k == FAR:
            relay_visual(1)
        if k == TILES + 2 and nh > 2:
            relay_visual(2)

    def wait_hops(some):
        for way in (lead, 1 - lead):
            for t, c in some:

                @pl.when(jnp.logical_and(rank(way) < t, rank(way) >= starts(t, c)))
                def _():
                    hop(way, block_of(way, t), c).wait_send()

    for j in range(3, nh):
        relay_visual(j)
    forward(agl, ag_sems, on_sems.at[2])
    if staged:
        forward_ahead()
    wait_rest(agl, ag_sems)
    for i in range(2):
        kgb[i] = agl[:, i].reshape(n * rows, cols).astype(BF16)
    for i in range(3):
        take_visual(i)
    wait_all(qgl, qg_sems)
    for s in range(n):
        part, block = s % split, s // split
        qg_out[
            part * text_part : (part + 1) * text_part, block * width : (block + 1) * width
        ] = qgl[s]
    if staged:
        add_ahead()
    for i in range(3, len(UNITS) - 1):
        take_visual(i)
    for copy in sends:
        copy.wait_send()
    wait_hops(order[: 2 * TILES])
    take_visual(len(UNITS) - 1)

    for c in range(TILES):
        at = slice(c * tile, (c + 1) * tile)
        vg_out[:, at] = vgp[my_head, c]
        for way in (lead, 1 - lead):
            t = rank(way)
            count = jnp.where(t == nh - 1, FAR, NEAR)

            @pl.when(t > jnp.where(c < count, 1, 0))
            def _():
                hop(way, my_head, c).wait_recv()
                vg_out[:, at] += zz[way, my_head, c]

    wait_hops(order[2 * TILES :])
    for way in (lead, 1 - lead):
        if staged:

            @pl.when(rank(way) < nh - 1)
            def _():
                kg_hop(way, True).wait_send()

    if staged:

        @pl.when(is_end)
        def _():
            for k in range(len(staged)):
                for b in range(len(direct)):
                    stage_copy(k, b).wait_send()

    for way in range(2):
        for j in range(nh):
            s = my_head - j if way == 0 else my_head + j

            @pl.when(jnp.logical_and(jnp.logical_and(s >= 0, s < nh), can_go(way)))
            def _():
                quarter_copy(way, jnp.clip(s, 0, nh - 1)).wait_send()

    for copy in late:
        copy.wait_send()


def store(*refs):
    outs, sems = refs[len(refs) // 2 : -1], refs[-1]
    copies = []
    for i, (src, dst) in enumerate(zip(refs, outs)):
        step = src.shape[0] // STORES
        for k in range(STORES):
            at = pl.ds(k * step, step)
            copies.append(pltpu.make_async_copy(src.at[at], dst.at[at], sems.at[i, k]))
    for copy in copies:
        copy.start()
    for copy in copies:
        copy.wait()


def solution(mesh):
    n, nh = mesh.shape["frame"], mesh.shape["head"]

    def body(visual, w_key, w_value, queries, out_grad):
        rows, depth = visual.shape
        cols = w_key.shape[1]
        text, query_cols = queries.shape
        local_heads = query_cols // HEAD_DIM
        split = max(1, n // local_heads)
        part, width = text // split, query_cols * split // n
        vmem = pl.BlockSpec(memory_space=pltpu.VMEM)
        hbm = pl.BlockSpec(memory_space=pl.ANY)
        dn, dh = depth // n, depth // nh
        tile = dh // TILES
        slots = max(FAR, 2 * NEAR, 1)
        pairs = pltpu.SemaphoreType.DMA((2, n))
        dma = pltpu.SemaphoreType.DMA
        outs = pl.pallas_call(
            functools.partial(kernel, n, nh),
            out_shape=(
                pltpu.VMEM((text, query_cols), F32),
                pltpu.VMEM((dn, cols), F32),
                pltpu.VMEM((dn, cols), F32),
                pltpu.VMEM((rows, dh), F32),
            ),
            in_specs=[hbm] * 5,
            out_specs=(vmem,) * 4,
            scratch_shapes=[
                pltpu.VMEM((rows, depth), BF16),
                pltpu.VMEM((text, query_cols), F32),
                pltpu.VMEM((text, query_cols), F32),
                pltpu.VMEM((depth, cols), BF16),
                pltpu.VMEM((depth, cols), BF16),
                pltpu.VMEM((n, dn, rows), F32),
                pltpu.VMEM((n, dn, rows), F32),
                pltpu.VMEM((dn, n * rows), BF16),
                pltpu.VMEM((n, part, width), F32),
                pltpu.VMEM((n, part, width), F32),
                pltpu.VMEM((2, cols // HEAD_DIM, rows, HEAD_DIM), F32),
                pltpu.VMEM((2, n, rows, HEAD_DIM), F32),
                pltpu.VMEM((2, 2, n // 2, rows, HEAD_DIM), F32),
                pltpu.VMEM((2, n // 2, rows, HEAD_DIM), F32),
                pltpu.VMEM((2, n // 2, rows, HEAD_DIM), F32),
                pltpu.VMEM((2, rows, cols), F32),
                pltpu.VMEM((n, 2, rows, cols), F32),
                pltpu.VMEM((2, n * rows, cols), BF16),
                pltpu.VMEM((n, part, width), F32),
                pltpu.VMEM((n, part, width), F32),
                pltpu.VMEM((nh, TILES, rows, tile), F32),
                pltpu.VMEM((2, nh, TILES, rows, tile), F32),
                pltpu.VMEM((max(FAR + NEAR * (nh - 2), 1), 2, 2, tile // n, cols), F32),
                pltpu.VMEM((n, slots, 2, tile // n, cols), F32),
                pltpu.VMEM((2, 2, rows, cols), F32),
                pltpu.VMEM((width // HEAD_DIM, 2, n * rows, part * n), BF16),
                dma((3,)),
                dma((2, CHUNKS)),
                pairs, pairs,
                dma((2, 2, n)),
                dma((len(UNITS), 2, n)),
                dma((2, 2, nh)),
                dma((2, 2)),
                dma((2, 2, n // 2)),
                pairs, pairs,
                dma((4, n)),
                dma((2, 2, nh, TILES)),
                dma((max(FAR + NEAR * (nh - 2), 1), 2)),
                dma((2, slots)),
                pairs,
                dma((2, 2)),
                dma((2, n // 2)),
            ],
            compiler_params=pltpu.CompilerParams(
                collective_id=0, has_side_effects=True, vmem_limit_bytes=60000000
            ),
        )(visual, w_key, w_value, queries, out_grad)
        return pl.pallas_call(
            store,
            out_shape=tuple(jax.ShapeDtypeStruct(o.shape, o.dtype) for o in outs),
            in_specs=[vmem] * 4,
            out_specs=(hbm,) * 4,
            scratch_shapes=[dma((4, STORES))],
            compiler_params=pltpu.CompilerParams(vmem_limit_bytes=1 << 20),
        )(*[pltpu.with_memory_space_constraint(o, pltpu.VMEM) for o in outs])

    return jax.shard_map(
        body,
        mesh=mesh,
        in_specs=(
            P("frame", None),
            P(None, "head"),
            P(None, "head"),
            P("frame", "head"),
            P("frame", "head"),
        ),
        out_specs=(P("frame", "head"), P("frame", "head"), P("frame", "head"), P("frame", "head")),
        check_vma=False,
    )
```
